32 devices in a mesh: frag: 4 (over y, core), band: 8 (over z, x).
Axes of the slice: x: 2, y: 2, z: 4, core: 2. Of those that a mesh axis runs over, the one named last changes fastest.
Arguments:
- wave_coeffs: bfloat16 [4, 256, 262144], P('frag', 'band'), may hold values from -40 to 40
- old_potential: float32 [4, 262144], P('frag'), may hold values from -4 to 4
- occupations: float32 [4, 256], P('frag'), may hold values from 0 to 2
- box_sizes: int32 [4, 3], replicated, may hold values from 32 to 64, as said below
- box_offsets: int32 [4, 3], replicated, may hold values from 0 to 96, as said below
- patch_signs: int32 [4], replicated, may hold values from -1 to 1, as said below
Outputs:
- new_waves: bfloat16 [4, 256, 262144], P('frag', 'band')
- box_potential: float32 [4, 262144], P('frag')
- total_potential: float32 [128, 128, 128], P('band')
The draws below stay inside these ranges and needn't reach their ends.
Inputs may be any that keep to these rules, and one draw needn't show every extreme that they name: `box_sizes`: each entry is 32, 48 or 64. box_offsets + box_sizes <= 128 in every dimension. `patch_signs`: each entry is -1 or 1.
All inputs are finite; a program needn't handle non-finite values.
Results may differ from the reference program's by a relative error of at most 0.0065.
Values may be sent and summed in bfloat16 or wider, within the bound.
A program may use at most 384 MiB of HBM per device.

```python
import jax
import jax.numpy as jnp
from jax import lax

NB = 256
BOX = 64
G = 128
NS_ITERS = 8
FRAGS = 4
N_BAND = 8


def box_layout(key):
    size_key = jax.random.fold_in(key, 11)
    offset_key = jax.random.fold_in(key, 12)
    levels = jax.random.randint(size_key, (FRAGS, 3), 0, 3)
    levels = levels.at[0, :].set(2)
    levels = levels.at[1, :].set(0)
    levels = levels.at[2, 0].set(0)
    box_sizes = BOX // 4 * (2 + levels)
    raw_offsets = jax.random.randint(offset_key, (FRAGS, 3), 0, G - BOX // 2 + 1)
    offsets = raw_offsets % (G - box_sizes + 1)
    offsets = offsets.at[0, 0].set(0)
    offsets = offsets.at[1, 0].set(G - BOX // 2)
    offsets = offsets.at[2, 0].set(G // N_BAND)
    return (box_sizes.astype(jnp.int32), offsets.astype(jnp.int32))


def draw_box_sizes(key, part):
    return box_layout(key)[0]


def draw_box_offsets(key, part):
    return box_layout(key)[1]


def draw_patch_signs(key, part):
    signs = 2 * jax.random.randint(jax.random.fold_in(key, 21), (FRAGS,), 0, 2) - 1
    signs = signs.at[0].set(1)
    signs = signs.at[1].set(-1)
    return signs.astype(jnp.int32)


def draw_wave_coeffs(key, part):
    scale_key = jax.random.fold_in(key, 31)
    value_key = jax.random.fold_in(key, 32)
    scales = jnp.exp(jax.random.uniform(scale_key, (FRAGS, NB, 1), jnp.float32, 0.0, jnp.log(10.0)))
    values = scales * jnp.clip(jax.random.normal(value_key, (FRAGS, NB, BOX ** 3), jnp.float32), -4.0, 4.0)
    return values.astype(jnp.bfloat16)


def level_of(own_key, extent, shards, least, largest):
    factor_of = 1.0
    for axis_at, blocks in shards:
        heights = jax.random.uniform(jax.random.fold_in(jax.random.fold_in(own_key, 6), axis_at), (blocks,), jnp.float32, least / len(shards), largest / len(shards))
        factor_of = factor_of * jnp.repeat(jnp.exp(heights), extent[axis_at] // blocks).reshape((-1,) + (1,) * (len(extent) - 1 - axis_at))
    return factor_of


def noise(own_key, shape, deviation, reach, shards=(), kind=jnp.bfloat16):
    entries = deviation * jax.random.normal(own_key, shape, jnp.float32)
    if shards:
        entries = entries * level_of(own_key, shape, shards, -0.22, 0.18)
    return jnp.clip(entries, -reach, reach).astype(kind)


def setup_inputs(seed: int = 0) -> dict:
    seeds = jax.random.split(jax.random.key(seed), 7)
    wave_coeffs = draw_wave_coeffs(jax.random.fold_in(seeds[6], 71), 0)
    old_potential = noise(seeds[1], (FRAGS, BOX**3), 1.0, 4.0, ((0, 4),), jnp.float32)
    occupations = jnp.clip(2.0 * jax.random.uniform(seeds[2], (FRAGS, NB), jnp.float32) ** level_of(seeds[2], (FRAGS, NB), ((0, 4),), -0.2, 0.2), 0.0, 2.0)
    box_sizes = draw_box_sizes(jax.random.fold_in(seeds[6], 71), 0)
    box_offsets = draw_box_offsets(jax.random.fold_in(seeds[6], 71), 0)
    patch_signs = draw_patch_signs(jax.random.fold_in(seeds[6], 71), 0)
    return {"wave_coeffs": wave_coeffs, "old_potential": old_potential, "occupations": occupations, "box_sizes": box_sizes, "box_offsets": box_offsets, "patch_signs": patch_signs}


step_size = 0.1
screening = 0.5
local_factor = 0.75
epsilon = 1e-06

def box_mask(box_size):
    coords = jnp.arange(BOX).astype(jnp.int32)
    along_x = (coords < box_size[0]).astype(jnp.float32)
    along_y = (coords < box_size[1]).astype(jnp.float32)
    along_z = (coords < box_size[2]).astype(jnp.float32)
    return (along_x[:, None, None] * along_y[None, :, None] * along_z[None, None, :]).reshape(BOX * BOX * BOX)

def sine_table():
    index = jnp.arange(G).astype(jnp.float32) + 1.0
    table = jnp.sqrt(2.0 / (G + 1)) * jnp.sin(jnp.pi * index[:, None] * index[None, :] / (G + 1))
    eigen = 2.0 - 2.0 * jnp.cos(jnp.pi * index / (G + 1))
    return (table, eigen)

def newton_schulz(gram):
    highest = lax.Precision.HIGHEST
    frobenius = jnp.sqrt(jnp.sum(gram * gram) + epsilon)
    identity = jnp.eye(NB, dtype=jnp.float32)
    square_part = gram / frobenius
    inverse_part = identity
    for sweep in range(NS_ITERS):
        newton_step = 0.5 * (3.0 * identity - jnp.dot(inverse_part, square_part, precision=highest, preferred_element_type=jnp.float32))
        square_part = jnp.dot(square_part, newton_step, precision=highest, preferred_element_type=jnp.float32)
        inverse_part = jnp.dot(newton_step, inverse_part, precision=highest, preferred_element_type=jnp.float32)
    return (inverse_part / jnp.sqrt(frobenius)).astype(jnp.bfloat16)

def reference(wave_coeffs, old_potential, occupations, box_sizes, box_offsets, patch_signs):
    highest = lax.Precision.HIGHEST
    cell_volume = 1.0 / BOX ** 3
    table, eigen = sine_table()
    fresh_list = []
    patched = jnp.zeros((G, G, G), jnp.float32)
    for fragment in range(FRAGS):
        mask = box_mask(box_sizes[fragment])
        waves = wave_coeffs[fragment].astype(jnp.float32) * mask[None, :]
        cube = waves.reshape(NB, BOX, BOX, BOX)
        padded = jnp.pad(cube, ((0, 0), (1, 1), (1, 1), (1, 1)))
        beside = padded[:, 2:, 1:-1, 1:-1] + padded[:, :-2, 1:-1, 1:-1]
        beside = beside + padded[:, 1:-1, 2:, 1:-1] + padded[:, 1:-1, :-2, 1:-1]
        beside = beside + padded[:, 1:-1, 1:-1, 2:] + padded[:, 1:-1, 1:-1, :-2]
        kinetic = (6.0 * cube - beside).reshape(NB, BOX * BOX * BOX)
        applied = 0.5 * kinetic + old_potential[fragment][None, :] * waves
        trial = (mask[None, :] * (waves - step_size * applied)).astype(jnp.bfloat16)
        gram = lax.dot_general(trial, trial, (((1,), (1,)), ((), ())), preferred_element_type=jnp.float32) * cell_volume
        coeff = newton_schulz(gram)
        fresh = lax.dot_general(coeff, trial, (((0,), (0,)), ((), ())), preferred_element_type=jnp.float32)
        fresh_list.append(fresh.astype(jnp.bfloat16))
        density = lax.optimization_barrier(jnp.sum(occupations[fragment][:, None] * fresh * fresh, axis=0)) / NB
        frame = jnp.zeros((G + BOX, G + BOX, G + BOX), jnp.float32)
        start = box_offsets[fragment].astype(jnp.int32)
        frame = lax.dynamic_update_slice(frame, density.reshape(BOX, BOX, BOX), (start[0], start[1], start[2]))
        patched = patched + patch_signs[fragment].astype(jnp.float32) * frame[:G, :G, :G]
    spectrum = jnp.einsum('abc,ci->abi', patched, table, precision=highest)
    spectrum = jnp.einsum('abc,bi->aic', spectrum, table, precision=highest)
    spectrum = jnp.einsum('abc,ai->ibc', spectrum, table, precision=highest)
    spectrum = spectrum * (screening / (eigen[:, None, None] + eigen[None, :, None] + eigen[None, None, :] + screening))
    spectrum = jnp.einsum('abc,ai->ibc', spectrum, table, precision=highest)
    spectrum = jnp.einsum('abc,bi->aic', spectrum, table, precision=highest)
    hartree = jnp.einsum('abc,ci->abi', spectrum, table, precision=highest)
    total_potential = hartree - local_factor * jnp.cbrt(jnp.maximum(patched, 0.0))
    extended = jnp.pad(total_potential, ((0, BOX), (0, BOX), (0, BOX)))
    windows = []
    for fragment in range(FRAGS):
        mask = box_mask(box_sizes[fragment])
        start = box_offsets[fragment].astype(jnp.int32)
        window = lax.dynamic_slice(extended, (start[0], start[1], start[2]), (BOX, BOX, BOX))
        windows.append(window.reshape(BOX * BOX * BOX) * mask)
    return (jnp.stack(fresh_list), jnp.stack(windows), total_potential)
```

```python
import functools

import jax
import jax.numpy as jnp
from jax import lax
from jax.experimental import pallas as pl
from jax.experimental.pallas import tpu as pltpu
from jax.sharding import PartitionSpec as P

NB = 256
BOX = 64
G = 128
NS_ITERS = 8


step_size = 0.1
screening = 0.5
local_factor = 0.75
epsilon = 1e-06


def sine_table():
    index = jnp.arange(G).astype(jnp.float32) + 1.0
    table = jnp.sqrt(2.0 / (G + 1)) * jnp.sin(jnp.pi * index[:, None] * index[None, :] / (G + 1))
    eigen = 2.0 - 2.0 * jnp.cos(jnp.pi * index / (G + 1))
    return (table, eigen)


def newton_schulz(gram):
    highest = lax.Precision.HIGHEST
    frobenius = jnp.sqrt(jnp.sum(gram * gram) + epsilon)
    identity = jnp.eye(NB, dtype=jnp.float32)
    square_part = gram / frobenius
    inverse_part = identity
    for sweep in range(NS_ITERS):
        newton_step = 0.5 * (
            3.0 * identity
            - jnp.dot(
                inverse_part, square_part, precision=highest, preferred_element_type=jnp.float32
            )
        )
        square_part = jnp.dot(
            square_part, newton_step, precision=highest, preferred_element_type=jnp.float32
        )
        inverse_part = jnp.dot(
            newton_step, inverse_part, precision=highest, preferred_element_type=jnp.float32
        )
    return (inverse_part / jnp.sqrt(frobenius)).astype(jnp.bfloat16)


GROUP = 8 * BOX
LANES = 128
BLOCK = 256


def step_plan(band_count):
    return (2, 1) if 16 % band_count == 0 else (1, 2)


def live_units(sizes, band_count):
    planes, parts = step_plan(band_count)
    unit = jnp.arange(BOX // planes * parts, dtype=jnp.int32)
    per_device = sizes[0] * parts // (planes * band_count)
    owner = jnp.minimum(unit // per_device, band_count - 1)
    return (owner, unit % per_device)


def trial_kernel(planes, parts, sizes, owner, local, prev, main, after, potential, stencil, out, held):
    step, part = pl.program_id(0), pl.program_id(1)
    size_x, size_y, size_z = sizes[0], sizes[1], sizes[2]
    plane_cells = BOX * BOX
    span = plane_cells // parts
    place = local[step * parts + part]
    groups = size_y // (8 * parts)
    rows = out.shape[1]
    start = part * groups * GROUP if parts > 1 else 0
    live_end = size_y * BOX
    blocks = span // BLOCK

    def at(ref, first, offset, lanes):
        if parts > 1:
            offset = pl.multiple_of(start + offset, LANES)
        return ref[:, pl.ds(first + offset, lanes)]

    def chunk(p, offset):
        if parts == 1:
            if not 0 <= offset < plane_cells:
                return jnp.zeros((rows, LANES), jnp.bfloat16)
            value = main[:, pl.ds(p * plane_cells + offset, LANES)]
            if offset < span // 2:
                return value
            return jnp.where(offset < live_end, value, jnp.zeros_like(value))
        lane = start + offset
        inside = (lane >= 0) & (lane < live_end)
        lane = pl.multiple_of(jnp.clip(lane, 0, plane_cells - LANES), LANES)
        value = main[:, pl.ds(p * plane_cells + lane, LANES)]
        return jnp.where(inside, value, jnp.zeros_like(value))

    def in_plane(p):
        chunks = [chunk(p, k * LANES) for k in range(-1, span // LANES + 1)]
        windows = [jnp.concatenate(chunks[2 * b : 2 * b + 4], axis=1) for b in range(blocks)]
        if rows % 16:
            windows = [window.astype(jnp.float32) for window in windows]
        stacked = jnp.concatenate(windows, axis=0).astype(jnp.bfloat16)
        return jnp.dot(stacked, stencil[...], preferred_element_type=jnp.float32)

    def trial_block(p, beside, b, below_on, above_on):
        plane_cells_at = p * plane_cells
        offset = b * BLOCK
        below, below_at = (prev, 0) if p == 0 else (main, plane_cells_at - plane_cells)
        above, above_at = (after, 0) if p == planes - 1 else (main, plane_cells_at + plane_cells)
        v = at(main, plane_cells_at, offset, BLOCK).astype(jnp.float32)
        total = beside[b * rows : (b + 1) * rows, :]
        total = total + below_on * at(below, below_at, offset, BLOCK).astype(jnp.float32)
        total = total + above_on * at(above, above_at, offset, BLOCK).astype(jnp.float32)
        own = (1.0 - 3.0 * step_size) - step_size * at(potential, plane_cells_at, offset, BLOCK)
        return own * v + (0.5 * step_size) * total

    def ends(p):
        x = step * planes + p
        return (jnp.where(x > 0, 1.0, 0.0), jnp.where(x + 1 < size_x, 1.0, 0.0))

    @pl.when((step * planes < size_x) & (size_z == BOX))
    def _():
        for p in range(planes):
            beside = in_plane(p)
            below_on, above_on = ends(p)
            target = (place * planes + p) * groups * GROUP
            for first, last in ((0, blocks // 2), (blocks // 2, blocks * 3 // 4), (blocks * 3 // 4, blocks)):

                @pl.when(first * BLOCK < groups * GROUP)
                def _(first=first, last=last):
                    for b in range(first, last):
                        lane = pl.multiple_of(target + b * BLOCK, LANES)
                        value = trial_block(p, beside, b, below_on, above_on)
                        out[0, :, pl.ds(lane, BLOCK)] = value.astype(out.dtype)

    @pl.when((step * planes < size_x) & (size_z < BOX))
    def _():
        z = lax.rem(lax.broadcasted_iota(jnp.int32, (rows, LANES), 1), BOX)
        for p in range(planes):
            beside = in_plane(p)
            below_on, above_on = ends(p)
            for b in range(blocks):
                held[:, b * BLOCK : (b + 1) * BLOCK] = trial_block(p, beside, b, below_on, above_on)

            def group_step(group, carry):
                base = group * GROUP
                target = ((place * planes + p) * groups + group) * (8 * size_z)

                def load(k):
                    return held[:, pl.ds(pl.multiple_of(base + k * LANES, LANES), LANES)]

                def store(k, value):
                    lane = pl.multiple_of(target + k * LANES, LANES)
                    out[0, :, pl.ds(lane, LANES)] = value.astype(out.dtype)

                @pl.when(size_z == 48)
                def _():
                    last = load(3)
                    for k in range(3):
                        store(k, jnp.where(z < 48, load(k), pltpu.roll(last, 48 - 16 * k, 1)))

                @pl.when(size_z == 32)
                def _():
                    for k in range(2):
                        filler = pltpu.roll(load(2 * k + 1), 32, 1)
                        store(k, jnp.where(z < 32, load(2 * k), filler))

                return carry

            lax.fori_loop(0, groups, group_step, 0)


def in_plane_stencil(size_z):
    source = jnp.arange(2 * BLOCK)[:, None] - LANES
    target = jnp.arange(BLOCK)[None, :]
    along_y = jnp.abs(source - target) == BOX
    along_z = (jnp.abs(source - target) == 1) & ((source + LANES) // BOX == (target + LANES) // BOX)
    return ((along_y | along_z) & ((source + LANES) % BOX < size_z)).astype(jnp.bfloat16)


def packed_trial(wave, potential, stencil, sizes, owner, local, width, band_count):
    rows = wave.shape[0]
    planes, parts = step_plan(band_count)
    plane_cells = BOX * BOX

    def plane(step, sizes, shift):
        return jnp.clip(step * planes + shift, 0, sizes[0] - 1)

    def whole(i, j, sizes, owner, local):
        return (0, jnp.minimum(i, sizes[0] // planes - 1))

    return pl.pallas_call(
        functools.partial(trial_kernel, planes, parts),
        out_shape=jax.ShapeDtypeStruct((band_count, rows, width), jnp.bfloat16),
        grid_spec=pltpu.PrefetchScalarGridSpec(
            num_scalar_prefetch=3,
            grid=(BOX // planes, parts),
            in_specs=[
                pl.BlockSpec((rows, plane_cells), lambda i, j, s, o, l: (0, plane(i, s, -1))),
                pl.BlockSpec((rows, planes * plane_cells), whole),
                pl.BlockSpec((rows, plane_cells), lambda i, j, s, o, l: (0, plane(i, s, planes))),
                pl.BlockSpec((1, planes * plane_cells), whole),
                pl.BlockSpec((2 * BLOCK, BLOCK), lambda i, j, s, o, l: (0, 0)),
            ],
            out_specs=pl.BlockSpec(
                (1, rows, width), lambda i, j, s, o, l: (o[i * parts + j], 0, 0)
            ),
            scratch_shapes=[pltpu.VMEM((rows, plane_cells // parts), jnp.float32)],
        ),
        compiler_params=pltpu.CompilerParams(vmem_limit_bytes=40 << 20),
        name="packed_trial",
    )(sizes, owner, local, wave, wave, wave, potential, stencil)


def unpack_kernel(planes, parts, plane_cells, sizes, owner, local, packed, out):
    step, part = pl.program_id(0), pl.program_id(1)
    size_x, size_y, size_z = sizes[0], sizes[1], sizes[2]
    place = local[step * parts + part]
    groups = size_y // (8 * parts)
    rows = out.shape[0]
    band_rows = min(rows, 16)
    z = lax.rem(lax.broadcasted_iota(jnp.int32, (band_rows, LANES), 1), BOX)
    live = step * planes < size_x
    source = place * planes * groups * (8 * size_z)

    @pl.when((part == 0) & ((size_y * BOX < plane_cells) | ~live))
    def _():
        def clear(k, carry):
            out[:, pl.ds(pl.multiple_of(k * GROUP, GROUP), GROUP)] = jnp.zeros(
                (rows, GROUP), out.dtype
            )
            return carry

        lax.fori_loop(0, planes * plane_cells // GROUP, clear, 0)

    @pl.when(live & (size_z == BOX))
    def _():
        for p in range(planes):

            def group_copy(group, carry):
                base = pl.multiple_of(p * plane_cells + (part * groups + group) * GROUP, GROUP)
                at = pl.multiple_of(source + (p * groups + group) * GROUP, GROUP)
                out[:, pl.ds(base, GROUP)] = packed[0, :, pl.ds(at, GROUP)]
                return carry

            lax.fori_loop(0, groups, group_copy, 0)

    @pl.when(live & (size_z < BOX))
    def _():
        for p in range(planes):

            def group_step(group, carry):
                base = p * plane_cells + (part * groups + group) * GROUP
                origin = source + (p * groups + group) * (8 * size_z)
                for first in range(0, rows, band_rows):
                    band = slice(first, first + band_rows)

                    def load(k):
                        at = pl.multiple_of(origin + k * LANES, LANES)
                        return packed[0, band, pl.ds(at, LANES)].astype(jnp.float32)

                    def store(k, value):
                        at = pl.multiple_of(base + k * LANES, LANES)
                        out[band, pl.ds(at, LANES)] = value.astype(out.dtype)

                    @pl.when(size_z == 48)
                    def _():
                        last = jnp.zeros((band_rows, LANES), jnp.float32)
                        for k in range(3):
                            value = load(k)
                            store(k, jnp.where(z < 48, value, 0.0))
                            mine = (z >= 16 * k) & (z < 16 * k + 16)
                            last = jnp.where(mine, pltpu.roll(value, 80 + 16 * k, 1), last)
                        store(3, last)

                    @pl.when(size_z == 32)
                    def _():
                        for k in range(2):
                            value = load(k)
                            store(2 * k, jnp.where(z < 32, value, 0.0))
                            store(2 * k + 1, jnp.where(z < 32, pltpu.roll(value, 96, 1), 0.0))

                return carry

            lax.fori_loop(0, groups, group_step, 0)


def unpacked(packed, sizes, owner, local, steps, planes, parts, plane_cells):
    count, rows, width = packed.shape
    return pl.pallas_call(
        functools.partial(unpack_kernel, planes, parts, plane_cells),
        out_shape=jax.ShapeDtypeStruct((rows, steps * planes * plane_cells), packed.dtype),
        grid_spec=pltpu.PrefetchScalarGridSpec(
            num_scalar_prefetch=3,
            grid=(steps, parts),
            in_specs=[
                pl.BlockSpec((1, rows, width), lambda i, j, s, o, l: (o[i * parts + j], 0, 0))
            ],
            out_specs=pl.BlockSpec((rows, planes * plane_cells), lambda i, j, s, o, l: (0, i)),
        ),
        compiler_params=pltpu.CompilerParams(vmem_limit_bytes=40 << 20),
        name="unpacked",
    )(sizes, owner, local, packed)


def summed(partial_value, band_count):
    blocks = partial_value.reshape(band_count, NB // band_count, NB)
    blocks = lax.all_to_all(blocks, "band", split_axis=0, concat_axis=0, tiled=True)
    mine = jnp.sum(blocks, axis=0)
    return gathered(mine, band_count).reshape(NB, NB)


def gathered(block, band_count):
    copies = jnp.broadcast_to(block[None], (band_count,) + block.shape)
    return lax.all_to_all(copies, "band", split_axis=0, concat_axis=0, tiled=True)


def hits(position, extent):
    return position[..., None] == jnp.arange(extent)


def patched_grid(shares, box_sizes, box_offsets, patch_signs, planes, parts):
    band_count, slots = shares.shape[1:3]
    per_device = (box_sizes[:, 0] * parts // (planes * band_count))[:, None, None, None]
    place = jnp.arange(slots)[None, None, :, None]
    unit = jnp.arange(band_count)[None, :, None, None] * per_device + place
    plane = jnp.arange(planes)[None, None, None, :]
    x = jnp.where(place < per_device, unit * planes // parts + plane, -G)
    x = x + box_offsets[:, 0][:, None, None, None]
    depth = BOX // parts
    y = jnp.arange(depth)[None, :]
    along_z = hits(box_offsets[:, 2][:, None] + jnp.arange(BOX)[None, :], G)
    fragments = box_sizes.shape[0]
    cube = shares.reshape(fragments, -1, depth, BOX)
    half = jnp.bfloat16
    wide = lax.dot_general(
        cube, along_z.astype(half), (((3,), (1,)), ((0,), (0,))), preferred_element_type=half
    )
    total = 0.0
    for part in range(parts):
        own = jnp.where(unit % parts == part, x, -G).reshape(fragments, -1)
        along_x = hits(own, G) * patch_signs[:, None, None]
        length = (box_sizes[:, 1] // parts)[:, None]
        row = jnp.where(y < length, box_offsets[:, 1][:, None] + part * length + y, -G)
        along_y = hits(row, G).astype(half)
        flat = lax.dot_general(
            wide, along_y, (((2,), (1,)), ((0,), (0,))), preferred_element_type=half
        )
        total = total + lax.dot_general(
            along_x.astype(half), flat, (((0, 1), (0, 1)), ((), ())), preferred_element_type=jnp.float32
        )
    return total.transpose(0, 2, 1)


def potential_of(patched):
    table, eigen = sine_table()
    precise = lax.Precision.HIGH
    spectrum = jnp.einsum("abc,ci->abi", patched, table, precision=precise)
    spectrum = jnp.einsum("abc,bi->aic", spectrum, table, precision=precise)
    spectrum = jnp.einsum("abc,ai->ibc", spectrum, table, precision=precise)
    spectrum = spectrum * (
        screening
        / (eigen[:, None, None] + eigen[None, :, None] + eigen[None, None, :] + screening)
    )
    spectrum = jnp.einsum("abc,ai->ibc", spectrum, table, precision=precise)
    spectrum = jnp.einsum("abc,bi->aic", spectrum, table, precision=precise)
    hartree = jnp.einsum("abc,ci->abi", spectrum, table, precision=precise)
    return hartree - local_factor * jnp.cbrt(jnp.maximum(patched, 0.0))


def body(wave_coeffs, old_potential, occupations, box_sizes, box_offsets, patch_signs):
    fragment = lax.axis_index("frag")
    band_index = lax.axis_index("band")
    band_count = lax.axis_size("band")
    frag_count = lax.axis_size("frag")
    planes, parts = step_plan(band_count)
    cells = BOX * BOX * BOX
    cell_volume = 1.0 / BOX**3
    sizes_here = lax.dynamic_index_in_dim(box_sizes, fragment, 0, keepdims=False)
    offsets_here = lax.dynamic_index_in_dim(box_offsets, fragment, 0, keepdims=False)
    axis = jnp.arange(BOX)
    mask = (
        (axis < sizes_here[0])[:, None, None]
        & (axis < sizes_here[1])[None, :, None]
        & (axis < sizes_here[2])[None, None, :]
    )
    owner, local = live_units(sizes_here, band_count)
    room = cells // band_count
    lengths = (BOX // 2, BOX * 3 // 4, BOX)
    widths = sorted({a * b * c // band_count for a in lengths for b in lengths for c in lengths})
    widths = widths[::-1]
    width_here = sizes_here[0] * sizes_here[1] * sizes_here[2] // band_count
    choice = jnp.sum((width_here < jnp.array(widths)).astype(jnp.int32))
    unit_cells = BOX * BOX // parts
    slots = room // (planes * unit_cells)
    stencil = in_plane_stencil(sizes_here[2])
    share_sizes = jnp.stack(
        [sizes_here[0] * parts // band_count, sizes_here[1] // parts, sizes_here[2]]
    )
    share_owner = jnp.zeros(slots, jnp.int32)
    share_local = jnp.arange(slots, dtype=jnp.int32)

    def forward(width):
        def branch(wave, potential, occupied):
            trial = packed_trial(
                wave, potential, stencil, sizes_here, owner, local, width, band_count
            )
            rows = lax.all_to_all(trial, "band", split_axis=0, concat_axis=0, tiled=True)
            rows = rows.reshape(NB, width)
            partial_value = lax.dot_general(
                rows, rows, (((1,), (1,)), ((), ())), preferred_element_type=jnp.float32
            )
            gram = summed(partial_value, band_count) * cell_volume
            coeff = newton_schulz(gram)
            fresh = lax.dot_general(
                coeff, rows, (((0,), (0,)), ((), ())), preferred_element_type=jnp.float32
            )
            density = jnp.sum(occupied[0][:, None] * fresh * fresh, axis=0) / NB
            sent = fresh.astype(jnp.bfloat16).reshape(band_count, NB // band_count, width)
            share = unpacked(
                density.astype(jnp.bfloat16).reshape(1, 1, width),
                share_sizes,
                share_owner,
                share_local,
                slots,
                planes,
                1,
                unit_cells,
            )
            return (jnp.pad(sent, ((0, 0), (0, 0), (0, room - width))), share[0])

        return branch

    sent, share = lax.switch(
        choice, [forward(width) for width in widths], wave_coeffs[0], old_potential, occupations
    )
    shares = lax.all_gather(share, ("frag", "band"), axis=0, tiled=False)
    shares = shares.reshape(frag_count, band_count, slots, planes, -1)

    def backward(width):
        def branch(sent, shares):
            back = lax.all_to_all(
                sent[:, :, :width], "band", split_axis=0, concat_axis=0, tiled=True
            )
            patched = patched_grid(shares, box_sizes, box_offsets, patch_signs, planes, parts)
            total_potential = potential_of(patched)
            slab_rows = G // band_count
            slab = lax.dynamic_slice_in_dim(total_potential, band_index * slab_rows, slab_rows)
            extended = jnp.pad(total_potential, ((0, BOX), (0, BOX), (0, BOX)))
            window = lax.dynamic_slice(
                extended, (offsets_here[0], offsets_here[1], offsets_here[2]), (BOX, BOX, BOX)
            )
            window = jnp.where(mask, window, 0.0).reshape(1, cells)
            waves_out = unpacked(
                back, sizes_here, owner, local, BOX // planes, planes, parts, BOX * BOX
            )
            return (waves_out[None], window, slab)

        return branch

    return lax.switch(choice, [backward(width) for width in widths], sent, shares)


def solution(mesh):
    placed = (P("frag", "band", None), P("frag", None), P("frag", None), P(), P(), P())
    return jax.shard_map(
        body,
        mesh=mesh,
        in_specs=placed,
        out_specs=(P("frag", "band", None), P("frag", None), P("band", None, None)),
        check_vma=False,
    )
```

```python
import functools

import jax
import jax.numpy as jnp
from jax import lax
from jax.experimental import pallas as pl
from jax.experimental.pallas import tpu as pltpu
from jax.sharding import PartitionSpec as P

NB = 256
BOX = 64
G = 128
NS_ITERS = 8


step_size = 0.1
screening = 0.5
local_factor = 0.75
epsilon = 1e-06


def sine_table():
    index = jnp.arange(G).astype(jnp.float32) + 1.0
    table = jnp.sqrt(2.0 / (G + 1)) * jnp.sin(jnp.pi * index[:, None] * index[None, :] / (G + 1))
    eigen = 2.0 - 2.0 * jnp.cos(jnp.pi * index / (G + 1))
    return (table, eigen)


def newton_schulz(gram):
    highest = lax.Precision.HIGHEST
    frobenius = jnp.sqrt(jnp.sum(gram * gram) + epsilon)
    identity = jnp.eye(NB, dtype=jnp.float32)
    square_part = gram / frobenius
    inverse_part = identity
    for sweep in range(NS_ITERS):
        newton_step = 0.5 * (
            3.0 * identity
            - jnp.dot(
                inverse_part, square_part, precision=highest, preferred_element_type=jnp.float32
            )
        )
        square_part = jnp.dot(
            square_part, newton_step, precision=highest, preferred_element_type=jnp.float32
        )
        inverse_part = jnp.dot(
            newton_step, inverse_part, precision=highest, preferred_element_type=jnp.float32
        )
    return (inverse_part / jnp.sqrt(frobenius)).astype(jnp.bfloat16)


GROUP = 8 * BOX
LANES = 128
BLOCK = 256


def step_plan(band_count):
    return (2, 1) if 16 % band_count == 0 else (1, 2)


CLASSES = (64, 48, 36, 18, 8)


def units_per_device(size_x, band_count):
    planes, parts = step_plan(band_count)
    return size_x * parts // (planes * band_count)


def live_units(sizes, band_count):
    planes, parts = step_plan(band_count)
    unit = jnp.arange(BOX // planes * parts, dtype=jnp.int32)
    per_device = units_per_device(sizes[0], band_count)
    owner = jnp.minimum(unit // per_device, band_count - 1)
    return (owner, unit % per_device)


def class_widths(band_count):
    planes, parts = step_plan(band_count)
    lengths = (BOX // 2, BOX * 3 // 4, BOX)
    widths = []
    for top, below in zip(CLASSES, CLASSES[1:] + (0,)):
        first, rest = 0, 0
        for x in lengths:
            for y in lengths:
                for z in lengths:
                    if below * BOX**3 < x * y * z * 64 <= top * BOX**3:
                        unit = planes * y * z // parts
                        first = max(first, unit)
                        rest = max(rest, (units_per_device(x, band_count) - 1) * unit)
        widths.append((first, rest))
    return widths


def trial_kernel(planes, parts, first_place, sizes, prev, main, after, potential, stencil, out, held):
    band_count = pl.num_programs(0)
    per_device = units_per_device(sizes[0], band_count)
    index = pl.program_id(1)
    unit = pl.program_id(0) * per_device + first_place + index
    step, part = unit // parts, unit % parts
    live = first_place + index < per_device
    size_x, size_y, size_z = sizes[0], sizes[1], sizes[2]
    plane_cells = BOX * BOX
    span = plane_cells // parts
    groups = size_y // (8 * parts)
    rows, width = out.shape[1:]
    start = part * groups * GROUP if parts > 1 else 0
    live_end = size_y * BOX
    blocks = span // BLOCK

    def at(ref, first, offset, lanes):
        if parts > 1:
            offset = pl.multiple_of(start + offset, LANES)
        return ref[:, pl.ds(first + offset, lanes)]

    def chunk(p, offset):
        if parts == 1:
            if not 0 <= offset < plane_cells:
                return jnp.zeros((rows, LANES), jnp.bfloat16)
            value = main[:, pl.ds(p * plane_cells + offset, LANES)]
            if offset < span // 2:
                return value
            return jnp.where(offset < live_end, value, jnp.zeros_like(value))
        lane = start + offset
        inside = (lane >= 0) & (lane < live_end)
        lane = pl.multiple_of(jnp.clip(lane, 0, plane_cells - LANES), LANES)
        value = main[:, pl.ds(p * plane_cells + lane, LANES)]
        return jnp.where(inside, value, jnp.zeros_like(value))

    def in_plane(p):
        chunks = [chunk(p, k * LANES) for k in range(-1, span // LANES + 1)]
        windows = [jnp.concatenate(chunks[2 * b : 2 * b + 4], axis=1) for b in range(blocks)]
        if rows % 16:
            windows = [window.astype(jnp.float32) for window in windows]
        stacked = jnp.concatenate(windows, axis=0).astype(jnp.bfloat16)
        return jnp.dot(stacked, stencil[...], preferred_element_type=jnp.float32)

    def trial_block(p, beside, b, below_on, above_on):
        plane_cells_at = p * plane_cells
        offset = b * BLOCK
        below, below_at = (prev, 0) if p == 0 else (main, plane_cells_at - plane_cells)
        above, above_at = (after, 0) if p == planes - 1 else (main, plane_cells_at + plane_cells)
        v = at(main, plane_cells_at, offset, BLOCK).astype(jnp.float32)
        total = beside[b * rows : (b + 1) * rows, :]
        total = total + below_on * at(below, below_at, offset, BLOCK).astype(jnp.float32)
        total = total + above_on * at(above, above_at, offset, BLOCK).astype(jnp.float32)
        own = (1.0 - 3.0 * step_size) - step_size * at(potential, plane_cells_at, offset, BLOCK)
        return own * v + (0.5 * step_size) * total

    def ends(p):
        x = step * planes + p
        return (jnp.where(x > 0, 1.0, 0.0), jnp.where(x + 1 < size_x, 1.0, 0.0))

    @pl.when(index == 0)
    def _():
        filled = jnp.clip(per_device - first_place, 0, pl.num_programs(1))
        filled = filled * planes * groups * (8 * size_z)

        def clear(k, carry):
            lane = pl.multiple_of(k * LANES, LANES)
            out[0, :, pl.ds(lane, LANES)] = jnp.zeros((rows, LANES), out.dtype)
            return carry

        lax.fori_loop(filled // LANES, width // LANES, clear, 0)

    @pl.when(live & (size_z == BOX))
    def _():
        for p in range(planes):
            beside = in_plane(p)
            below_on, above_on = ends(p)
            target = (index * planes + p) * groups * GROUP
            for first, last in ((0, blocks // 2), (blocks // 2, blocks * 3 // 4), (blocks * 3 // 4, blocks)):

                @pl.when(first * BLOCK < groups * GROUP)
                def _(first=first, last=last):
                    for b in range(first, last):
                        lane = pl.multiple_of(target + b * BLOCK, LANES)
                        value = trial_block(p, beside, b, below_on, above_on)
                        out[0, :, pl.ds(lane, BLOCK)] = value.astype(out.dtype)

    @pl.when(live & (size_z < BOX))
    def _():
        z = lax.rem(lax.broadcasted_iota(jnp.int32, (rows, LANES), 1), BOX)
        for p in range(planes):
            beside = in_plane(p)
            below_on, above_on = ends(p)
            for b in range(blocks):
                held[:, b * BLOCK : (b + 1) * BLOCK] = trial_block(p, beside, b, below_on, above_on)

            def group_step(group, carry):
                base = group * GROUP
                target = ((index * planes + p) * groups + group) * (8 * size_z)

                def load(k):
                    return held[:, pl.ds(pl.multiple_of(base + k * LANES, LANES), LANES)]

                def store(k, value):
                    lane = pl.multiple_of(target + k * LANES, LANES)
                    out[0, :, pl.ds(lane, LANES)] = value.astype(out.dtype)

                @pl.when(size_z == 48)
                def _():
                    last = load(3)
                    for k in range(3):
                        store(k, jnp.where(z < 48, load(k), pltpu.roll(last, 48 - 16 * k, 1)))

                @pl.when(size_z == 32)
                def _():
                    for k in range(2):
                        filler = pltpu.roll(load(2 * k + 1), 32, 1)
                        store(k, jnp.where(z < 32, load(2 * k), filler))

                return carry

            lax.fori_loop(0, groups, group_step, 0)


def in_plane_stencil(size_z):
    source = jnp.arange(2 * BLOCK)[:, None] - LANES
    target = jnp.arange(BLOCK)[None, :]
    along_y = jnp.abs(source - target) == BOX
    along_z = (jnp.abs(source - target) == 1) & ((source + LANES) // BOX == (target + LANES) // BOX)
    return ((along_y | along_z) & ((source + LANES) % BOX < size_z)).astype(jnp.bfloat16)


def packed_trial(wave, potential, stencil, sizes, first_place, places, width, band_count):
    rows = wave.shape[0]
    planes, parts = step_plan(band_count)
    plane_cells = BOX * BOX

    def step(i, j, sizes):
        per_device = units_per_device(sizes[0], band_count)
        return (i * per_device + jnp.minimum(first_place + j, per_device - 1)) // parts

    def plane(shift):
        return lambda i, j, s: (0, jnp.clip(step(i, j, s) * planes + shift, 0, s[0] - 1))

    share = places * planes * plane_cells * band_count // parts
    return pl.pallas_call(
        functools.partial(trial_kernel, planes, parts, first_place),
        out_shape=jax.ShapeDtypeStruct((band_count, rows, width), jnp.bfloat16),
        grid_spec=pltpu.PrefetchScalarGridSpec(
            num_scalar_prefetch=1,
            grid=(band_count, places),
            in_specs=[
                pl.BlockSpec((rows, plane_cells), plane(-1)),
                pl.BlockSpec((rows, planes * plane_cells), lambda i, j, s: (0, step(i, j, s))),
                pl.BlockSpec((rows, plane_cells), plane(planes)),
                pl.BlockSpec((1, planes * plane_cells), lambda i, j, s: (0, step(i, j, s))),
                pl.BlockSpec((2 * BLOCK, BLOCK), lambda i, j, s: (0, 0)),
            ],
            out_specs=pl.BlockSpec((1, rows, width), lambda i, j, s: (i, 0, 0)),
            scratch_shapes=[pltpu.VMEM((rows, plane_cells // parts), jnp.float32)],
        ),
        compiler_params=pltpu.CompilerParams(vmem_limit_bytes=40 << 20),
        cost_estimate=pl.CostEstimate(
            flops=1024 * rows * share, bytes_accessed=6 * rows * share, transcendentals=0
        ),
        name="packed_trial",
    )(sizes, wave, wave, wave, potential, stencil)


def unpack_kernel(planes, parts, plane_cells, sizes, owner, local, head, tail, out):
    step, part = pl.program_id(0), pl.program_id(1)
    size_x, size_y, size_z = sizes[0], sizes[1], sizes[2]
    place = local[step * parts + part]
    groups = size_y // (8 * parts)
    rows = out.shape[0]
    band_rows = min(rows, 16)
    z = lax.rem(lax.broadcasted_iota(jnp.int32, (band_rows, LANES), 1), BOX)
    live = step * planes < size_x
    source = jnp.maximum(place - 1, 0) * planes * groups * (8 * size_z)

    @pl.when((part == 0) & ((size_y * BOX < plane_cells) | ~live))
    def _():
        def clear(k, carry):
            out[:, pl.ds(pl.multiple_of(k * GROUP, GROUP), GROUP)] = jnp.zeros(
                (rows, GROUP), out.dtype
            )
            return carry

        lax.fori_loop(0, planes * plane_cells // GROUP, clear, 0)

    def copy_from(packed):
        for p in range(planes):

            def group_copy(group, carry):
                base = pl.multiple_of(p * plane_cells + (part * groups + group) * GROUP, GROUP)
                at = pl.multiple_of(source + (p * groups + group) * GROUP, GROUP)
                out[:, pl.ds(base, GROUP)] = packed[0, :, pl.ds(at, GROUP)]
                return carry

            lax.fori_loop(0, groups, group_copy, 0)

    def spread_from(packed):
        for p in range(planes):

            def group_step(group, carry):
                base = p * plane_cells + (part * groups + group) * GROUP
                origin = source + (p * groups + group) * (8 * size_z)
                for first in range(0, rows, band_rows):
                    band = slice(first, first + band_rows)

                    def load(k):
                        at = pl.multiple_of(origin + k * LANES, LANES)
                        return packed[0, band, pl.ds(at, LANES)].astype(jnp.float32)

                    def store(k, value):
                        at = pl.multiple_of(base + k * LANES, LANES)
                        out[band, pl.ds(at, LANES)] = value.astype(out.dtype)

                    @pl.when(size_z == 48)
                    def _():
                        last = jnp.zeros((band_rows, LANES), jnp.float32)
                        for k in range(3):
                            value = load(k)
                            store(k, jnp.where(z < 48, value, 0.0))
                            mine = (z >= 16 * k) & (z < 16 * k + 16)
                            last = jnp.where(mine, pltpu.roll(value, 80 + 16 * k, 1), last)
                        store(3, last)

                    @pl.when(size_z == 32)
                    def _():
                        for k in range(2):
                            value = load(k)
                            store(2 * k, jnp.where(z < 32, value, 0.0))
                            store(2 * k + 1, jnp.where(z < 32, pltpu.roll(value, 96, 1), 0.0))

                return carry

            lax.fori_loop(0, groups, group_step, 0)

    for packed, chosen in ((head, place == 0), (tail, place > 0)):
        pl.when(live & chosen & (size_z == BOX))(functools.partial(copy_from, packed))
        pl.when(live & chosen & (size_z < BOX))(functools.partial(spread_from, packed))


def unpacked(head, tail, sizes, owner, local, steps, planes, parts, plane_cells):
    rows = head.shape[1]

    def owned(i, j, s, o, l):
        return (o[i * parts + j], 0, 0)

    return pl.pallas_call(
        functools.partial(unpack_kernel, planes, parts, plane_cells),
        out_shape=jax.ShapeDtypeStruct((rows, steps * planes * plane_cells), head.dtype),
        grid_spec=pltpu.PrefetchScalarGridSpec(
            num_scalar_prefetch=3,
            grid=(steps, parts),
            in_specs=[
                pl.BlockSpec((1, rows, head.shape[2]), owned),
                pl.BlockSpec((1, rows, tail.shape[2]), owned),
            ],
            out_specs=pl.BlockSpec((rows, planes * plane_cells), lambda i, j, s, o, l: (0, i)),
        ),
        compiler_params=pltpu.CompilerParams(vmem_limit_bytes=40 << 20),
        cost_estimate=pl.CostEstimate(
            flops=0, bytes_accessed=4 * rows * steps * planes * plane_cells, transcendentals=0
        ),
        name="unpacked",
    )(sizes, owner, local, head, tail)


def summed(partial_value, band_count):
    blocks = partial_value.reshape(band_count, NB // band_count, NB)
    blocks = lax.all_to_all(blocks, "band", split_axis=0, concat_axis=0, tiled=True)
    mine = jnp.sum(blocks, axis=0)
    return gathered(mine, band_count).reshape(NB, NB)


def gathered(block, band_count):
    copies = jnp.broadcast_to(block[None], (band_count,) + block.shape)
    return lax.all_to_all(copies, "band", split_axis=0, concat_axis=0, tiled=True)


def hits(position, extent):
    return position[..., None] == jnp.arange(extent)


def patched_grid(shares, box_sizes, box_offsets, patch_signs, band_count, slots, planes, parts):
    per_device = units_per_device(box_sizes[:, 0], band_count)[:, None, None, None]
    place = jnp.arange(slots)[None, None, :, None]
    unit = jnp.arange(band_count)[None, :, None, None] * per_device + place
    plane = jnp.arange(planes)[None, None, None, :]
    x = jnp.where(place < per_device, unit * planes // parts + plane, -G)
    x = x + box_offsets[:, 0][:, None, None, None]
    pair = LANES // BOX
    depth = BOX // (parts * pair)
    y = jnp.arange(depth)[None, :] * pair
    lane = jnp.arange(LANES)[None, :]
    fragments = box_sizes.shape[0]
    half = jnp.bfloat16
    cube = shares.reshape(fragments, -1, LANES)
    slabs, rows_of = [], []
    for odd in range(pair):
        z = jnp.where(lane // BOX == odd, box_offsets[:, 2][:, None] + lane % BOX, -G)
        along_z = hits(z, G).astype(half)
        wide = lax.dot_general(
            cube, along_z, (((2,), (1,)), ((0,), (0,))), preferred_element_type=half
        ).reshape(fragments, -1, depth, G)
        for part in range(parts):
            own = jnp.where(unit % parts == part, x, -G).reshape(fragments, -1)
            along_x = (hits(own, G) * patch_signs[:, None, None]).astype(half)
            slabs.append(
                lax.dot_general(
                    along_x, wide, (((1,), (1,)), ((0,), (0,))), preferred_element_type=half
                )
            )
            length = (box_sizes[:, 1] // parts)[:, None]
            row = box_offsets[:, 1][:, None] + part * length + y + odd
            rows_of.append(hits(jnp.where(y + odd < length, row, -G), G).astype(half))
    total = lax.dot_general(
        jnp.stack(rows_of, 1),
        jnp.stack(slabs, 1),
        (((0, 1, 2), (0, 1, 3)), ((), ())),
        preferred_element_type=jnp.float32,
    )
    return total.transpose(1, 0, 2)


def hartree_of(patched, table, eigen):
    precise = lax.Precision.HIGH
    spectrum = jnp.einsum("abc,ci->abi", patched, table, precision=precise)
    spectrum = jnp.einsum("abc,bi->aic", spectrum, table, precision=precise)
    spectrum = jnp.einsum("abc,ai->ibc", spectrum, table, precision=precise)
    spectrum = spectrum * (
        screening
        / (eigen[:, None, None] + eigen[None, :, None] + eigen[None, None, :] + screening)
    )
    spectrum = jnp.einsum("abc,ai->ibc", spectrum, table, precision=precise)
    spectrum = jnp.einsum("abc,bi->aic", spectrum, table, precision=precise)
    return jnp.einsum("abc,ci->abi", spectrum, table, precision=precise)


def total_of(hartree, patched):
    return hartree - local_factor * jnp.cbrt(jnp.maximum(patched, 0.0))


def widened(block, width):
    return jnp.pad(block, ((0, 0),) * (block.ndim - 1) + ((0, width - block.shape[-1]),))


def swapped(blocks):
    return lax.all_to_all(blocks, "band", split_axis=0, concat_axis=0, tiled=True)


def body(wave_coeffs, old_potential, occupations, box_sizes, box_offsets, patch_signs):
    fragment = lax.axis_index("frag")
    band_index = lax.axis_index("band")
    band_count = lax.axis_size("band")
    planes, parts = step_plan(band_count)
    cells = BOX * BOX * BOX
    cell_volume = 1.0 / BOX**3
    sizes_here = lax.dynamic_index_in_dim(box_sizes, fragment, 0, keepdims=False)
    offsets_here = lax.dynamic_index_in_dim(box_offsets, fragment, 0, keepdims=False)
    axis = jnp.arange(BOX)
    mask = (
        (axis < sizes_here[0])[:, None, None]
        & (axis < sizes_here[1])[None, :, None]
        & (axis < sizes_here[2])[None, None, :]
    )
    owner, local = live_units(sizes_here, band_count)
    widths = class_widths(band_count)
    room = tuple(max(pair) for pair in zip(*widths))
    volume = sizes_here[0] * sizes_here[1] * sizes_here[2] * 64
    tops = jnp.array([top * BOX**3 for top in CLASSES], jnp.int32)
    choice = jnp.sum((volume <= tops).astype(jnp.int32)) - 1
    unit_cells = BOX * BOX // parts
    slots = units_per_device(BOX, band_count)
    share_sizes = jnp.stack(
        [units_per_device(sizes_here[0], band_count) * planes, sizes_here[1] // parts, sizes_here[2]]
    )
    share_owner = jnp.zeros(slots, jnp.int32)
    share_local = jnp.arange(slots, dtype=jnp.int32)

    def forward(pair):
        def branch(wave, potential):
            stencil = in_plane_stencil(sizes_here[2])
            rows, partial_value = [], 0.0
            places = ((0, 1), (1, slots - 1))
            for (first, count), width, space in zip(places, pair, room):
                trial = packed_trial(
                    wave, potential, stencil, sizes_here, first, count, width, band_count
                )
                part = swapped(trial).reshape(NB, width)
                partial_value = partial_value + lax.dot_general(
                    part, part, (((1,), (1,)), ((), ())), preferred_element_type=jnp.float32
                )
                rows.append(widened(part, space))
            return (rows[0], rows[1], partial_value)

        return branch

    head, tail, partial_value = lax.switch(
        choice, [forward(pair) for pair in widths], wave_coeffs[0], old_potential
    )
    gram = summed(partial_value, band_count) * cell_volume
    coeff = newton_schulz(gram)

    def middle(pair):
        def branch(head, tail, coeff, occupied):
            sent, density = [], []
            for rows, width, space in zip((head, tail), pair, room):
                fresh = lax.dot_general(
                    coeff,
                    rows[:, :width],
                    (((0,), (0,)), ((), ())),
                    preferred_element_type=jnp.float32,
                )
                value = jnp.sum(occupied[0][:, None] * fresh * fresh, axis=0) / NB
                density.append(value.astype(jnp.bfloat16).reshape(1, 1, width))
                fresh = fresh.astype(jnp.bfloat16)
                sent.append(widened(fresh.reshape(band_count, NB // band_count, width), space))
            share = unpacked(
                density[0],
                density[1],
                share_sizes,
                share_owner,
                share_local,
                slots,
                planes,
                1,
                unit_cells,
            )
            return (sent[0], sent[1], share.reshape(-1, LANES))

        return branch

    sent_head, sent_tail, share = lax.switch(
        choice, [middle(pair) for pair in widths], head, tail, coeff, occupations
    )
    shares = lax.all_gather(share, ("frag", "band"), axis=0, tiled=True)

    def early(pair):
        def branch(sent):
            return widened(swapped(sent[:, :, : pair[0]]), room[0])

        return branch

    back_head = lax.switch(choice, [early(pair) for pair in widths], sent_head)

    table, eigen = lax.optimization_barrier(sine_table())

    def late(pair):
        def branch(back_head, sent, shares):
            back = swapped(sent[:, :, : pair[1]])
            patched = patched_grid(
                shares, box_sizes, box_offsets, patch_signs, band_count, slots, planes, parts
            )
            hartree = hartree_of(patched, table, eigen)

            def slab_of(grid):
                rows = G // band_count
                return lax.dynamic_slice_in_dim(grid, band_index * rows, rows)

            def window_of(grid):
                extended = jnp.pad(grid, ((0, BOX), (0, BOX), (0, BOX)))
                return lax.dynamic_slice(
                    extended, (offsets_here[0], offsets_here[1], offsets_here[2]), (BOX, BOX, BOX)
                )

            slab = total_of(slab_of(hartree), slab_of(patched))
            window = total_of(window_of(hartree), window_of(patched))
            window = jnp.where(mask, window, 0.0).reshape(1, cells)
            waves_out = unpacked(
                back_head[:, :, : pair[0]],
                back,
                sizes_here,
                owner,
                local,
                BOX // planes,
                planes,
                parts,
                BOX * BOX,
            )
            return (waves_out[None], window, slab)

        return branch

    return lax.switch(
        choice, [late(pair) for pair in widths], back_head, sent_tail, shares
    )


def solution(mesh):
    placed = (P("frag", "band", None), P("frag", None), P("frag", None), P(), P(), P())
    return jax.shard_map(
        body,
        mesh=mesh,
        in_specs=placed,
        out_specs=(P("frag", "band", None), P("frag", None), P("band", None, None)),
        check_vma=False,
    )
```

```python
import functools

import jax
import jax.numpy as jnp
from jax import lax
from jax.experimental import pallas as pl
from jax.experimental.pallas import tpu as pltpu
from jax.sharding import PartitionSpec as P

NB = 256
BOX = 64
G = 128
NS_ITERS = 8


step_size = 0.1
screening = 0.5
local_factor = 0.75
epsilon = 1e-06


def sine_table():
    index = jnp.arange(G).astype(jnp.float32) + 1.0
    table = jnp.sqrt(2.0 / (G + 1)) * jnp.sin(jnp.pi * index[:, None] * index[None, :] / (G + 1))
    eigen = 2.0 - 2.0 * jnp.cos(jnp.pi * index / (G + 1))
    return (table, eigen)


def newton_schulz(gram):
    highest = lax.Precision.HIGHEST
    frobenius = jnp.sqrt(jnp.sum(gram * gram) + epsilon)
    identity = jnp.eye(NB, dtype=jnp.float32)
    square_part = gram / frobenius
    inverse_part = identity
    for sweep in range(NS_ITERS):
        newton_step = 0.5 * (
            3.0 * identity
            - jnp.dot(
                inverse_part, square_part, precision=highest, preferred_element_type=jnp.float32
            )
        )
        square_part = jnp.dot(
            square_part, newton_step, precision=highest, preferred_element_type=jnp.float32
        )
        inverse_part = jnp.dot(
            newton_step, inverse_part, precision=highest, preferred_element_type=jnp.float32
        )
    return (inverse_part / jnp.sqrt(frobenius)).astype(jnp.bfloat16)


GROUP = 8 * BOX
LANES = 128
BLOCK = 256


def step_plan(band_count):
    return (2, 1) if 16 % band_count == 0 else (1, 2)


CLASSES = (64, 48, 36, 32, 27, 18, 8)


def units_per_device(size_x, band_count):
    planes, parts = step_plan(band_count)
    return size_x * parts // (planes * band_count)


def live_units(sizes, band_count):
    planes, parts = step_plan(band_count)
    unit = jnp.arange(BOX // planes * parts, dtype=jnp.int32)
    per_device = units_per_device(sizes[0], band_count)
    owner = jnp.minimum(unit // per_device, band_count - 1)
    return (owner, unit % per_device)


def class_widths(band_count):
    planes, parts = step_plan(band_count)
    lengths = (BOX // 2, BOX * 3 // 4, BOX)
    widths = []
    for top, below in zip(CLASSES, CLASSES[1:] + (0,)):
        first, rest = 0, 0
        for x in lengths:
            for y in lengths:
                for z in lengths:
                    if below * BOX**3 < x * y * z * 64 <= top * BOX**3:
                        unit = planes * y * z // parts
                        first = max(first, unit)
                        rest = max(rest, (units_per_device(x, band_count) - 1) * unit)
        widths.append((first, rest))
    return widths


def trial_kernel(planes, parts, first_place, sizes, prev, main, after, potential, stencil, packing, out, held):
    band_count = pl.num_programs(0)
    per_device = units_per_device(sizes[0], band_count)
    index = pl.program_id(1)
    unit = pl.program_id(0) * per_device + first_place + index
    step, part = unit // parts, unit % parts
    live = first_place + index < per_device
    size_x, size_y, size_z = sizes[0], sizes[1], sizes[2]
    plane_cells = BOX * BOX
    span = plane_cells // parts
    groups = size_y // (8 * parts)
    rows, width = out.shape[1:]
    start = part * groups * GROUP if parts > 1 else 0
    live_end = size_y * BOX
    blocks = span // BLOCK

    def at(ref, first, offset, lanes):
        if parts > 1:
            offset = pl.multiple_of(start + offset, LANES)
        return ref[:, pl.ds(first + offset, lanes)]

    def chunk(p, offset):
        if parts == 1:
            if not 0 <= offset < plane_cells:
                return jnp.zeros((rows, LANES), jnp.bfloat16)
            value = main[:, pl.ds(p * plane_cells + offset, LANES)]
            if offset < span // 2:
                return value
            return jnp.where(offset < live_end, value, jnp.zeros_like(value))
        lane = start + offset
        inside = (lane >= 0) & (lane < live_end)
        lane = pl.multiple_of(jnp.clip(lane, 0, plane_cells - LANES), LANES)
        value = main[:, pl.ds(p * plane_cells + lane, LANES)]
        return jnp.where(inside, value, jnp.zeros_like(value))

    def in_plane(p):
        chunks = [chunk(p, k * LANES) for k in range(-1, span // LANES + 1)]
        windows = [jnp.concatenate(chunks[2 * b : 2 * b + 4], axis=1) for b in range(blocks)]
        return jnp.dot(stack(windows), stencil[...], preferred_element_type=jnp.float32)

    def trial_block(p, beside, b, below_on, above_on):
        plane_cells_at = p * plane_cells
        offset = b * BLOCK
        below, below_at = (prev, 0) if p == 0 else (main, plane_cells_at - plane_cells)
        above, above_at = (after, 0) if p == planes - 1 else (main, plane_cells_at + plane_cells)
        v = at(main, plane_cells_at, offset, BLOCK).astype(jnp.float32)
        total = beside[b * rows : (b + 1) * rows, :]
        total = total + below_on * at(below, below_at, offset, BLOCK).astype(jnp.float32)
        total = total + above_on * at(above, above_at, offset, BLOCK).astype(jnp.float32)
        own = (1.0 - 3.0 * step_size) - step_size * at(potential, plane_cells_at, offset, BLOCK)
        return own * v + (0.5 * step_size) * total

    def ends(p):
        x = step * planes + p
        return (jnp.where(x > 0, 1.0, 0.0), jnp.where(x + 1 < size_x, 1.0, 0.0))

    @pl.when(index == 0)
    def _():
        filled = jnp.clip(per_device - first_place, 0, pl.num_programs(1))
        filled = filled * planes * groups * (8 * size_z)

        def clear(k, carry):
            lane = pl.multiple_of(k * LANES, LANES)
            out[0, :, pl.ds(lane, LANES)] = jnp.zeros((rows, LANES), out.dtype)
            return carry

        lax.fori_loop(filled // LANES, width // LANES, clear, 0)

    depth = blocks * BLOCK // GROUP
    segments = ((0, depth // 2), (depth // 2, depth * 3 // 4), (depth * 3 // 4, depth))
    doubled = jnp.where(size_z == 32, 2, 1)

    @pl.when(live)
    def _():
        for p in range(planes):
            beside = in_plane(p)
            below_on, above_on = ends(p)
            target = (index * planes + p) * groups * (8 * size_z)
            for first, last in segments:

                @pl.when(first < groups)
                def _(first=first, last=last):
                    for b in range(first * GROUP // BLOCK, last * GROUP // BLOCK):
                        value = trial_block(p, beside, b, below_on, above_on)
                        held[:, b * BLOCK : (b + 1) * BLOCK] = value.astype(held.dtype)

            @pl.when(size_z == BOX)
            def _():
                def group_copy(group, carry):
                    lane = pl.multiple_of(target + group * GROUP, GROUP)
                    base = pl.multiple_of(group * GROUP, GROUP)
                    out[0, :, pl.ds(lane, GROUP)] = held[:, pl.ds(base, GROUP)]
                    return carry

                lax.fori_loop(0, groups, group_copy, 0)

            @pl.when(size_z < BOX)
            def _():
                for j in range(3):
                    begin = (j if j != 1 else doubled) * LANES
                    picked = []
                    for group in range(depth):
                        at_lane = begin + group * GROUP
                        if j == 1:
                            at_lane = pl.multiple_of(at_lane, LANES)
                        picked.append(held[:, pl.ds(at_lane, BLOCK)])
                    packed = jnp.dot(stack(picked), packing[j], preferred_element_type=jnp.float32)

                    @pl.when((size_z == 48) | (j < 2))
                    def _(j=j, packed=packed):
                        for first, last in segments:

                            @pl.when(first < groups)
                            def _(first=first, last=last):
                                for group in range(first, last):
                                    lane = target + group * (8 * size_z) + j * LANES
                                    lane = pl.multiple_of(lane, LANES)
                                    value = packed[group * rows : (group + 1) * rows, :]
                                    out[0, :, pl.ds(lane, LANES)] = value.astype(out.dtype)


def stack(pieces):
    if pieces[0].shape[0] % 16:
        pieces = [piece.astype(jnp.float32) for piece in pieces]
    return jnp.concatenate(pieces, axis=0).astype(jnp.bfloat16)


def packing_tables(size_z):
    j = jnp.arange(3)[:, None, None]
    k = jnp.arange(BLOCK)[None, :, None]
    lane = j * LANES + jnp.arange(LANES)[None, None, :]
    begin = jnp.where(size_z == 32, 2 * j, j) * LANES
    source = lane // size_z * BOX + lane % size_z - begin
    return ((source == k) & (lane < 8 * size_z)).astype(jnp.bfloat16)


def spreading_tables(size_z):
    i = jnp.arange(2)[:, None, None]
    k = jnp.arange(BLOCK)[None, :, None]
    lane = i * BLOCK + jnp.arange(BLOCK)[None, None, :]
    begin = jnp.where(size_z == 48, i, 0) * LANES
    source = lane // BOX * size_z + lane % BOX - begin
    return ((source == k) & (lane % BOX < size_z)).astype(jnp.bfloat16)


def in_plane_stencil(size_z):
    source = jnp.arange(2 * BLOCK)[:, None] - LANES
    target = jnp.arange(BLOCK)[None, :]
    along_y = jnp.abs(source - target) == BOX
    along_z = (jnp.abs(source - target) == 1) & ((source + LANES) // BOX == (target + LANES) // BOX)
    return ((along_y | along_z) & ((source + LANES) % BOX < size_z)).astype(jnp.bfloat16)


def packed_trial(wave, potential, stencil, packing, sizes, first_place, places, width, band_count):
    rows = wave.shape[0]
    planes, parts = step_plan(band_count)
    plane_cells = BOX * BOX

    def step(i, j, sizes):
        per_device = units_per_device(sizes[0], band_count)
        return (i * per_device + jnp.minimum(first_place + j, per_device - 1)) // parts

    def plane(shift):
        return lambda i, j, s: (0, jnp.clip(step(i, j, s) * planes + shift, 0, s[0] - 1))

    share = places * planes * plane_cells * band_count // parts
    return pl.pallas_call(
        functools.partial(trial_kernel, planes, parts, first_place),
        out_shape=jax.ShapeDtypeStruct((band_count, rows, width), jnp.bfloat16),
        grid_spec=pltpu.PrefetchScalarGridSpec(
            num_scalar_prefetch=1,
            grid=(band_count, places),
            in_specs=[
                pl.BlockSpec((rows, plane_cells), plane(-1)),
                pl.BlockSpec((rows, planes * plane_cells), lambda i, j, s: (0, step(i, j, s))),
                pl.BlockSpec((rows, plane_cells), plane(planes)),
                pl.BlockSpec((1, planes * plane_cells), lambda i, j, s: (0, step(i, j, s))),
                pl.BlockSpec((2 * BLOCK, BLOCK), lambda i, j, s: (0, 0)),
                pl.BlockSpec((3, BLOCK, LANES), lambda i, j, s: (0, 0, 0)),
            ],
            out_specs=pl.BlockSpec((1, rows, width), lambda i, j, s: (i, 0, 0)),
            scratch_shapes=[pltpu.VMEM((rows, plane_cells // parts), jnp.bfloat16)],
        ),
        compiler_params=pltpu.CompilerParams(vmem_limit_bytes=40 << 20),
        cost_estimate=pl.CostEstimate(
            flops=1024 * rows * share, bytes_accessed=6 * rows * share, transcendentals=0
        ),
        name="packed_trial",
    )(sizes, wave, wave, wave, potential, stencil, packing)


def unpack_kernel(planes, parts, plane_cells, sizes, owner, local, head, tail, spreading, out):
    step, part = pl.program_id(0), pl.program_id(1)
    size_x, size_y, size_z = sizes[0], sizes[1], sizes[2]
    place = local[step * parts + part]
    groups = size_y // (8 * parts)
    rows = out.shape[0]
    live = step * planes < size_x
    source = jnp.maximum(place - 1, 0) * planes * groups * (8 * size_z)

    @pl.when((part == 0) & ((size_y * BOX < plane_cells) | ~live))
    def _():
        def clear(k, carry):
            out[:, pl.ds(pl.multiple_of(k * GROUP, GROUP), GROUP)] = jnp.zeros(
                (rows, GROUP), out.dtype
            )
            return carry

        lax.fori_loop(0, planes * plane_cells // GROUP, clear, 0)

    def copy_from(packed):
        for p in range(planes):

            def group_copy(group, carry):
                base = pl.multiple_of(p * plane_cells + (part * groups + group) * GROUP, GROUP)
                at = pl.multiple_of(source + (p * groups + group) * GROUP, GROUP)
                out[:, pl.ds(base, GROUP)] = packed[0, :, pl.ds(at, GROUP)]
                return carry

            lax.fori_loop(0, groups, group_copy, 0)

    depth = plane_cells // (GROUP * parts)
    segments = ((0, depth // 2), (depth // 2, depth * 3 // 4), (depth * 3 // 4, depth))
    if depth % 4:
        segments = ((k, k + 1) for k in range(depth))

    def spread_from(packed):
        last_lane = packed.shape[2] - BLOCK
        for p in range(planes):
            for i in range(2):
                shift = jnp.where(size_z == 48, i, 0) * LANES
                picked = []
                for group in range(depth):
                    at = source + (p * groups + group) * (8 * size_z) + shift
                    at = pl.multiple_of(jnp.minimum(at, last_lane), LANES)
                    picked.append(packed[0, :, pl.ds(at, BLOCK)])
                spread = jnp.dot(stack(picked), spreading[i], preferred_element_type=jnp.float32)
                for first, last in segments:

                    @pl.when(first < groups)
                    def _(first=first, last=last, spread=spread, i=i, p=p):
                        for group in range(first, last):
                            lane = p * plane_cells + (part * groups + group) * GROUP + i * BLOCK
                            lane = pl.multiple_of(lane, BLOCK)
                            value = spread[group * rows : (group + 1) * rows, :]
                            out[:, pl.ds(lane, BLOCK)] = value.astype(out.dtype)

    for packed, chosen in ((head, place == 0), (tail, place > 0)):
        pl.when(live & chosen & (size_z == BOX))(functools.partial(copy_from, packed))
        pl.when(live & chosen & (size_z < BOX))(functools.partial(spread_from, packed))


def unpacked(head, tail, spreading, sizes, owner, local, steps, planes, parts, plane_cells):
    rows = head.shape[1]

    def owned(i, j, s, o, l):
        return (o[i * parts + j], 0, 0)

    return pl.pallas_call(
        functools.partial(unpack_kernel, planes, parts, plane_cells),
        out_shape=jax.ShapeDtypeStruct((rows, steps * planes * plane_cells), head.dtype),
        grid_spec=pltpu.PrefetchScalarGridSpec(
            num_scalar_prefetch=3,
            grid=(steps, parts),
            in_specs=[
                pl.BlockSpec((1, rows, head.shape[2]), owned),
                pl.BlockSpec((1, rows, tail.shape[2]), owned),
                pl.BlockSpec((2, BLOCK, BLOCK), lambda i, j, s, o, l: (0, 0, 0)),
            ],
            out_specs=pl.BlockSpec((rows, planes * plane_cells), lambda i, j, s, o, l: (0, i)),
        ),
        compiler_params=pltpu.CompilerParams(vmem_limit_bytes=40 << 20),
        cost_estimate=pl.CostEstimate(
            flops=0, bytes_accessed=4 * rows * steps * planes * plane_cells, transcendentals=0
        ),
        name="unpacked",
    )(sizes, owner, local, head, tail, spreading)


def summed(partial_value, band_count):
    blocks = partial_value.reshape(band_count, NB // band_count, NB)
    blocks = lax.all_to_all(blocks, "band", split_axis=0, concat_axis=0, tiled=True)
    mine = jnp.sum(blocks, axis=0)
    return gathered(mine, band_count).reshape(NB, NB)


def gathered(block, band_count):
    copies = jnp.broadcast_to(block[None], (band_count,) + block.shape)
    return lax.all_to_all(copies, "band", split_axis=0, concat_axis=0, tiled=True)


def hits(position, extent):
    return position[..., None] == jnp.arange(extent)


def patched_grid(shares, box_sizes, box_offsets, patch_signs, band_count, slots, planes, parts):
    per_device = units_per_device(box_sizes[:, 0], band_count)[:, None, None, None]
    place = jnp.arange(slots)[None, None, :, None]
    unit = jnp.arange(band_count)[None, :, None, None] * per_device + place
    plane = jnp.arange(planes)[None, None, None, :]
    x = jnp.where(place < per_device, unit * planes // parts + plane, -G)
    x = x + box_offsets[:, 0][:, None, None, None]
    pair = LANES // BOX
    depth = BOX // (parts * pair)
    y = jnp.arange(depth)[None, :] * pair
    lane = jnp.arange(LANES)[None, :]
    fragments = box_sizes.shape[0]
    half = jnp.bfloat16
    cube = shares.reshape(fragments, -1, LANES)
    slabs, rows_of = [], []
    for odd in range(pair):
        z = jnp.where(lane // BOX == odd, box_offsets[:, 2][:, None] + lane % BOX, -G)
        along_z = hits(z, G).astype(half)
        wide = lax.dot_general(
            cube, along_z, (((2,), (1,)), ((0,), (0,))), preferred_element_type=half
        ).reshape(fragments, -1, depth, G)
        for part in range(parts):
            own = jnp.where(unit % parts == part, x, -G).reshape(fragments, -1)
            along_x = (hits(own, G) * patch_signs[:, None, None]).astype(half)
            slabs.append(
                lax.dot_general(
                    along_x, wide, (((1,), (1,)), ((0,), (0,))), preferred_element_type=half
                )
            )
            length = (box_sizes[:, 1] // parts)[:, None]
            row = box_offsets[:, 1][:, None] + part * length + y + odd
            rows_of.append(hits(jnp.where(y + odd < length, row, -G), G).astype(half))
    total = lax.dot_general(
        jnp.stack(rows_of, 1),
        jnp.stack(slabs, 1),
        (((0, 1, 2), (0, 1, 3)), ((), ())),
        preferred_element_type=jnp.float32,
    )
    return total.transpose(1, 0, 2)


def hartree_of(patched, table, eigen):
    precise = lax.Precision.HIGH
    spectrum = jnp.einsum("abc,ci->abi", patched, table, precision=precise)
    spectrum = jnp.einsum("abc,bi->aic", spectrum, table, precision=precise)
    spectrum = jnp.einsum("abc,ai->ibc", spectrum, table, precision=precise)
    spectrum = spectrum * (
        screening
        / (eigen[:, None, None] + eigen[None, :, None] + eigen[None, None, :] + screening)
    )
    spectrum = jnp.einsum("abc,ai->ibc", spectrum, table, precision=precise)
    spectrum = jnp.einsum("abc,bi->aic", spectrum, table, precision=precise)
    return jnp.einsum("abc,ci->abi", spectrum, table, precision=precise)


def total_of(hartree, patched):
    return hartree - local_factor * jnp.cbrt(jnp.maximum(patched, 0.0))


def widened(block, width):
    return jnp.pad(block, ((0, 0),) * (block.ndim - 1) + ((0, width - block.shape[-1]),))


def swapped(blocks):
    return lax.all_to_all(blocks, "band", split_axis=0, concat_axis=0, tiled=True)


def body(wave_coeffs, old_potential, occupations, box_sizes, box_offsets, patch_signs):
    fragment = lax.axis_index("frag")
    band_index = lax.axis_index("band")
    band_count = lax.axis_size("band")
    planes, parts = step_plan(band_count)
    cells = BOX * BOX * BOX
    cell_volume = 1.0 / BOX**3
    sizes_here = lax.dynamic_index_in_dim(box_sizes, fragment, 0, keepdims=False)
    offsets_here = lax.dynamic_index_in_dim(box_offsets, fragment, 0, keepdims=False)
    axis = jnp.arange(BOX)
    mask = (
        (axis < sizes_here[0])[:, None, None]
        & (axis < sizes_here[1])[None, :, None]
        & (axis < sizes_here[2])[None, None, :]
    )
    owner, local = live_units(sizes_here, band_count)
    widths = class_widths(band_count)
    room = tuple(max(pair) for pair in zip(*widths))
    volume = sizes_here[0] * sizes_here[1] * sizes_here[2] * 64
    tops = jnp.array([top * BOX**3 for top in CLASSES], jnp.int32)
    choice = jnp.sum((volume <= tops).astype(jnp.int32)) - 1
    unit_cells = BOX * BOX // parts
    slots = units_per_device(BOX, band_count)
    share_sizes = jnp.stack(
        [units_per_device(sizes_here[0], band_count) * planes, sizes_here[1] // parts, sizes_here[2]]
    )
    share_owner = jnp.zeros(slots, jnp.int32)
    share_local = jnp.arange(slots, dtype=jnp.int32)

    stencil = in_plane_stencil(sizes_here[2])
    packing = packing_tables(sizes_here[2])
    spreading = spreading_tables(sizes_here[2])

    def forward(pair):
        def branch(wave, potential):
            rows, partial_value = [], 0.0
            places = ((0, 1), (1, slots - 1))
            for (first, count), width, space in zip(places, pair, room):
                trial = packed_trial(
                    wave, potential, stencil, packing, sizes_here, first, count, width, band_count
                )
                part = swapped(trial).reshape(NB, width)
                partial_value = partial_value + lax.dot_general(
                    part, part, (((1,), (1,)), ((), ())), preferred_element_type=jnp.float32
                )
                rows.append(widened(part, space))
            return (rows[0], rows[1], partial_value)

        return branch

    head, tail, partial_value = lax.switch(
        choice, [forward(pair) for pair in widths], wave_coeffs[0], old_potential
    )
    gram = summed(partial_value, band_count) * cell_volume
    coeff = newton_schulz(gram)

    sent, density = [], []
    for rows, width in zip((head, tail), room):
        fresh = lax.dot_general(
            coeff, rows, (((0,), (0,)), ((), ())), preferred_element_type=jnp.float32
        )
        value = jnp.sum(occupations[0][:, None] * fresh * fresh, axis=0) / NB
        density.append(jnp.broadcast_to(value.astype(jnp.bfloat16), (1, 8, width)))
        sent.append(fresh.astype(jnp.bfloat16).reshape(band_count, NB // band_count, width))
    sent_head, sent_tail = sent
    share = unpacked(
        density[0],
        density[1],
        spreading,
        share_sizes,
        share_owner,
        share_local,
        slots,
        planes,
        1,
        unit_cells,
    )
    share = share[0].reshape(-1, LANES)
    shares = lax.all_gather(share, ("frag", "band"), axis=0, tiled=True)

    def early(pair):
        def branch(sent):
            return widened(swapped(sent[:, :, : pair[0]]), room[0])

        return branch

    back_head = lax.switch(choice, [early(pair) for pair in widths], sent_head)

    table, eigen = lax.optimization_barrier(sine_table())

    rests = sorted({rest for _, rest in widths}, reverse=True)
    rests = [rest for k, rest in enumerate(rests) if k in (0, 1, 4, 6)]
    rest_here = (units_per_device(sizes_here[0], band_count) - 1) * planes
    rest_here = rest_here * (sizes_here[1] // parts) * sizes_here[2]
    late_choice = jnp.sum((rest_here <= jnp.array(rests)).astype(jnp.int32)) - 1

    def late(rest):
        def branch(sent, shares):
            back = swapped(sent[:, :, :rest])
            patched = patched_grid(
                shares, box_sizes, box_offsets, patch_signs, band_count, slots, planes, parts
            )
            hartree = hartree_of(patched, table, eigen)

            def slab_of(grid):
                rows = G // band_count
                return lax.dynamic_slice_in_dim(grid, band_index * rows, rows)

            def window_of(grid):
                extended = jnp.pad(grid, ((0, BOX), (0, BOX), (0, BOX)))
                return lax.dynamic_slice(
                    extended, (offsets_here[0], offsets_here[1], offsets_here[2]), (BOX, BOX, BOX)
                )

            slab = total_of(slab_of(hartree), slab_of(patched))
            window = total_of(window_of(hartree), window_of(patched))
            window = jnp.where(mask, window, 0.0).reshape(1, cells)
            return (widened(back, room[1]), window, slab)

        return branch

    back_tail, window, slab = lax.switch(
        late_choice, [late(rest) for rest in rests], sent_tail, shares
    )
    waves_out = unpacked(
        back_head,
        back_tail,
        spreading,
        sizes_here,
        owner,
        local,
        BOX // planes,
        planes,
        parts,
        BOX * BOX,
    )
    return (waves_out[None], window, slab)


def solution(mesh):
    placed = (P("frag", "band", None), P("frag", None), P("frag", None), P(), P(), P())
    return jax.shard_map(
        body,
        mesh=mesh,
        in_specs=placed,
        out_specs=(P("frag", "band", None), P("frag", None), P("band", None, None)),
        check_vma=False,
    )
```

```python
import functools

import jax
import jax.numpy as jnp
import numpy as np
from jax import lax
from jax.experimental import pallas as pl
from jax.experimental.pallas import tpu as pltpu
from jax.sharding import PartitionSpec as P

NB = 256
BOX = 64
G = 128
NS_ITERS = 8


step_size = 0.1
screening = 0.5
local_factor = 0.75
epsilon = 1e-06


def sine_table():
    index = jnp.arange(G).astype(jnp.float32) + 1.0
    table = jnp.sqrt(2.0 / (G + 1)) * jnp.sin(jnp.pi * index[:, None] * index[None, :] / (G + 1))
    eigen = 2.0 - 2.0 * jnp.cos(jnp.pi * index / (G + 1))
    return (table, eigen)


def newton_schulz(gram):
    highest = lax.Precision.HIGHEST
    frobenius = jnp.sqrt(jnp.sum(gram * gram) + epsilon)
    identity = jnp.eye(NB, dtype=jnp.float32)
    square_part = gram / frobenius
    inverse_part = identity
    for sweep in range(NS_ITERS):
        newton_step = 0.5 * (
            3.0 * identity
            - jnp.dot(
                inverse_part, square_part, precision=highest, preferred_element_type=jnp.float32
            )
        )
        square_part = jnp.dot(
            square_part, newton_step, precision=highest, preferred_element_type=jnp.float32
        )
        inverse_part = jnp.dot(
            newton_step, inverse_part, precision=highest, preferred_element_type=jnp.float32
        )
    return (inverse_part / jnp.sqrt(frobenius)).astype(jnp.bfloat16)


GROUP = 8 * BOX
LANES = 128
BLOCK = 256


def step_plan(band_count):
    return (2, 1) if 16 % band_count == 0 else (1, 2)


CLASSES = (64, 48, 36, 32, 27, 18, 8)


def units_per_device(size_x, band_count):
    planes, parts = step_plan(band_count)
    return size_x * parts // (planes * band_count)


def live_units(sizes, band_count):
    planes, parts = step_plan(band_count)
    unit = jnp.arange(BOX // planes * parts, dtype=jnp.int32)
    per_device = units_per_device(sizes[0], band_count)
    owner = jnp.minimum(unit // per_device, band_count - 1)
    return (owner, unit % per_device)


def class_widths(band_count):
    planes, parts = step_plan(band_count)
    lengths = (BOX // 2, BOX * 3 // 4, BOX)
    widths = []
    for top, below in zip(CLASSES, CLASSES[1:] + (0,)):
        first, rest = 0, 0
        for x in lengths:
            for y in lengths:
                for z in lengths:
                    if below * BOX**3 < x * y * z * 64 <= top * BOX**3:
                        unit = planes * y * z // parts
                        first = max(first, unit)
                        rest = max(rest, (units_per_device(x, band_count) - 1) * unit)
        widths.append((first, rest))
    return widths


def trial_kernel(planes, parts, first_place, sizes, prev, main, after, potential, stencil, packing, out, held):
    band_count = pl.num_programs(0)
    per_device = units_per_device(sizes[0], band_count)
    index = pl.program_id(1)
    unit = pl.program_id(0) * per_device + first_place + index
    step, part = unit // parts, unit % parts
    live = first_place + index < per_device
    size_x, size_y, size_z = sizes[0], sizes[1], sizes[2]
    plane_cells = BOX * BOX
    span = plane_cells // parts
    groups = size_y // (8 * parts)
    rows, width = out.shape[1:]
    start = part * groups * GROUP if parts > 1 else 0
    live_end = size_y * BOX
    blocks = span // BLOCK

    def at(ref, first, offset, lanes):
        if parts > 1:
            offset = pl.multiple_of(start + offset, LANES)
        return ref[:, pl.ds(first + offset, lanes)]

    def chunk(p, offset):
        if parts == 1:
            if not 0 <= offset < plane_cells:
                return jnp.zeros((rows, LANES), jnp.bfloat16)
            value = main[:, pl.ds(p * plane_cells + offset, LANES)]
            if offset < span // 2:
                return value
            return jnp.where(offset < live_end, value, jnp.zeros_like(value))
        lane = start + offset
        inside = (lane >= 0) & (lane < live_end)
        lane = pl.multiple_of(jnp.clip(lane, 0, plane_cells - LANES), LANES)
        value = main[:, pl.ds(p * plane_cells + lane, LANES)]
        return jnp.where(inside, value, jnp.zeros_like(value))

    def in_plane(p):
        chunks = [chunk(p, k * LANES) for k in range(-1, span // LANES + 1)]
        windows = [jnp.concatenate(chunks[2 * b : 2 * b + 4], axis=1) for b in range(blocks)]
        return jnp.dot(stack(windows), stencil[0], preferred_element_type=jnp.float32)

    def trial_block(p, beside, b, below_on, above_on):
        plane_cells_at = p * plane_cells
        offset = b * BLOCK
        below, below_at = (prev, 0) if p == 0 else (main, plane_cells_at - plane_cells)
        above, above_at = (after, 0) if p == planes - 1 else (main, plane_cells_at + plane_cells)
        v = at(main, plane_cells_at, offset, BLOCK).astype(jnp.float32)
        total = beside[b * rows : (b + 1) * rows, :]
        total = total + below_on * at(below, below_at, offset, BLOCK).astype(jnp.float32)
        total = total + above_on * at(above, above_at, offset, BLOCK).astype(jnp.float32)
        own = (1.0 - 3.0 * step_size) - step_size * at(potential, plane_cells_at, offset, BLOCK)
        return own * v + (0.5 * step_size) * total

    def ends(p):
        x = step * planes + p
        return (jnp.where(x > 0, 1.0, 0.0), jnp.where(x + 1 < size_x, 1.0, 0.0))

    @pl.when(index == 0)
    def _():
        filled = jnp.clip(per_device - first_place, 0, pl.num_programs(1))
        filled = filled * planes * groups * (8 * size_z)

        def clear(k, carry):
            lane = pl.multiple_of(k * LANES, LANES)
            out[0, :, pl.ds(lane, LANES)] = jnp.zeros((rows, LANES), out.dtype)
            return carry

        lax.fori_loop(filled // LANES, width // LANES, clear, 0)

    depth = blocks * BLOCK // GROUP
    segments = ((0, depth // 2), (depth // 2, depth * 3 // 4), (depth * 3 // 4, depth))
    doubled = jnp.where(size_z == 32, 2, 1)

    @pl.when(live)
    def _():
        for p in range(planes):
            beside = in_plane(p)
            below_on, above_on = ends(p)
            target = (index * planes + p) * groups * (8 * size_z)
            for first, last in segments:

                @pl.when(first < groups)
                def _(first=first, last=last):
                    for b in range(first * GROUP // BLOCK, last * GROUP // BLOCK):
                        value = trial_block(p, beside, b, below_on, above_on)
                        held[:, b * BLOCK : (b + 1) * BLOCK] = value.astype(held.dtype)

            @pl.when(size_z == BOX)
            def _():
                def group_copy(group, carry):
                    lane = pl.multiple_of(target + group * GROUP, GROUP)
                    base = pl.multiple_of(group * GROUP, GROUP)
                    out[0, :, pl.ds(lane, GROUP)] = held[:, pl.ds(base, GROUP)]
                    return carry

                lax.fori_loop(0, groups, group_copy, 0)

            @pl.when(size_z < BOX)
            def _():
                for j in range(3):
                    begin = (j if j != 1 else doubled) * LANES
                    picked = []
                    for group in range(depth):
                        at_lane = begin + group * GROUP
                        if j == 1:
                            at_lane = pl.multiple_of(at_lane, LANES)
                        picked.append(held[:, pl.ds(at_lane, BLOCK)])
                    packed = jnp.dot(stack(picked), packing[0, j], preferred_element_type=jnp.float32)

                    @pl.when((size_z == 48) | (j < 2))
                    def _(j=j, packed=packed):
                        for first, last in segments:

                            @pl.when(first < groups)
                            def _(first=first, last=last):
                                for group in range(first, last):
                                    lane = target + group * (8 * size_z) + j * LANES
                                    lane = pl.multiple_of(lane, LANES)
                                    value = packed[group * rows : (group + 1) * rows, :]
                                    out[0, :, pl.ds(lane, LANES)] = value.astype(out.dtype)


def stack(pieces):
    if pieces[0].shape[0] % 16:
        pieces = [piece.astype(jnp.float32) for piece in pieces]
    return jnp.concatenate(pieces, axis=0).astype(jnp.bfloat16)


def packing_table(size_z):
    j = np.arange(3)[:, None, None]
    k = np.arange(BLOCK)[None, :, None]
    lane = j * LANES + np.arange(LANES)[None, None, :]
    begin = (2 * j if size_z == 32 else j) * LANES
    source = lane // size_z * BOX + lane % size_z - begin
    return (source == k) & (lane < 8 * size_z)


def spreading_table(size_z):
    i = np.arange(2)[:, None, None]
    k = np.arange(BLOCK)[None, :, None]
    lane = i * BLOCK + np.arange(BLOCK)[None, None, :]
    begin = (i if size_z == 48 else 0) * LANES
    source = lane // BOX * size_z + lane % BOX - begin
    return (source == k) & (lane % BOX < size_z)


def in_plane_stencil(size_z):
    source = np.arange(2 * BLOCK)[:, None] - LANES
    target = np.arange(BLOCK)[None, :]
    along_y = np.abs(source - target) == BOX
    along_z = (np.abs(source - target) == 1) & ((source + LANES) // BOX == (target + LANES) // BOX)
    return (along_y | along_z) & ((source + LANES) % BOX < size_z)


def tables_of(make):
    return jnp.asarray(np.stack([make(z) for z in (32, 48, 64)]), jnp.bfloat16)


def level(size_z):
    return size_z // 16 - 2


def packed_trial(wave, potential, stencil, packing, sizes, first_place, places, width, band_count):
    rows = wave.shape[0]
    planes, parts = step_plan(band_count)
    plane_cells = BOX * BOX

    def step(i, j, sizes):
        per_device = units_per_device(sizes[0], band_count)
        return (i * per_device + jnp.minimum(first_place + j, per_device - 1)) // parts

    def plane(shift):
        return lambda i, j, s: (0, jnp.clip(step(i, j, s) * planes + shift, 0, s[0] - 1))

    share = places * planes * plane_cells * band_count // parts
    return pl.pallas_call(
        functools.partial(trial_kernel, planes, parts, first_place),
        out_shape=jax.ShapeDtypeStruct((band_count, rows, width), jnp.bfloat16),
        grid_spec=pltpu.PrefetchScalarGridSpec(
            num_scalar_prefetch=1,
            grid=(band_count, places),
            in_specs=[
                pl.BlockSpec((rows, plane_cells), plane(-1)),
                pl.BlockSpec((rows, planes * plane_cells), lambda i, j, s: (0, step(i, j, s))),
                pl.BlockSpec((rows, plane_cells), plane(planes)),
                pl.BlockSpec((1, planes * plane_cells), lambda i, j, s: (0, step(i, j, s))),
                pl.BlockSpec((1, 2 * BLOCK, BLOCK), lambda i, j, s: (level(s[2]), 0, 0)),
                pl.BlockSpec((1, 3, BLOCK, LANES), lambda i, j, s: (level(s[2]), 0, 0, 0)),
            ],
            out_specs=pl.BlockSpec((1, rows, width), lambda i, j, s: (i, 0, 0)),
            scratch_shapes=[pltpu.VMEM((rows, plane_cells // parts), jnp.bfloat16)],
        ),
        compiler_params=pltpu.CompilerParams(vmem_limit_bytes=40 << 20),
        cost_estimate=pl.CostEstimate(
            flops=1024 * rows * share, bytes_accessed=6 * rows * share, transcendentals=0
        ),
        name="packed_trial",
    )(sizes, wave, wave, wave, potential, stencil, packing)


def unpack_kernel(planes, parts, plane_cells, sizes, owner, local, head, tail, spreading, out):
    step, part = pl.program_id(0), pl.program_id(1)
    size_x, size_y, size_z = sizes[0], sizes[1], sizes[2]
    place = local[step * parts + part]
    groups = size_y // (8 * parts)
    rows = out.shape[0]
    live = step * planes < size_x
    source = jnp.maximum(place - 1, 0) * planes * groups * (8 * size_z)

    @pl.when((part == 0) & ((size_y * BOX < plane_cells) | ~live))
    def _():
        def clear(k, carry):
            out[:, pl.ds(pl.multiple_of(k * GROUP, GROUP), GROUP)] = jnp.zeros(
                (rows, GROUP), out.dtype
            )
            return carry

        lax.fori_loop(0, planes * plane_cells // GROUP, clear, 0)

    def copy_from(packed):
        for p in range(planes):

            def group_copy(group, carry):
                base = pl.multiple_of(p * plane_cells + (part * groups + group) * GROUP, GROUP)
                at = pl.multiple_of(source + (p * groups + group) * GROUP, GROUP)
                out[:, pl.ds(base, GROUP)] = packed[0, :, pl.ds(at, GROUP)]
                return carry

            lax.fori_loop(0, groups, group_copy, 0)

    depth = plane_cells // (GROUP * parts)
    segments = ((0, depth // 2), (depth // 2, depth * 3 // 4), (depth * 3 // 4, depth))
    if depth % 4:
        segments = ((k, k + 1) for k in range(depth))

    def spread_from(packed):
        last_lane = packed.shape[2] - BLOCK
        for p in range(planes):
            for i in range(2):
                shift = jnp.where(size_z == 48, i, 0) * LANES
                picked = []
                for group in range(depth):
                    at = source + (p * groups + group) * (8 * size_z) + shift
                    at = pl.multiple_of(jnp.minimum(at, last_lane), LANES)
                    picked.append(packed[0, :, pl.ds(at, BLOCK)])
                spread = jnp.dot(stack(picked), spreading[0, i], preferred_element_type=jnp.float32)
                for first, last in segments:

                    @pl.when(first < groups)
                    def _(first=first, last=last, spread=spread, i=i, p=p):
                        for group in range(first, last):
                            lane = p * plane_cells + (part * groups + group) * GROUP + i * BLOCK
                            lane = pl.multiple_of(lane, BLOCK)
                            value = spread[group * rows : (group + 1) * rows, :]
                            out[:, pl.ds(lane, BLOCK)] = value.astype(out.dtype)

    for packed, chosen in ((head, place == 0), (tail, place > 0)):
        pl.when(live & chosen & (size_z == BOX))(functools.partial(copy_from, packed))
        pl.when(live & chosen & (size_z < BOX))(functools.partial(spread_from, packed))


def unpacked(head, tail, spreading, sizes, owner, local, steps, planes, parts, plane_cells):
    rows = head.shape[1]

    def owned(i, j, s, o, l):
        return (o[i * parts + j], 0, 0)

    return pl.pallas_call(
        functools.partial(unpack_kernel, planes, parts, plane_cells),
        out_shape=jax.ShapeDtypeStruct((rows, steps * planes * plane_cells), head.dtype),
        grid_spec=pltpu.PrefetchScalarGridSpec(
            num_scalar_prefetch=3,
            grid=(steps, parts),
            in_specs=[
                pl.BlockSpec((1, rows, head.shape[2]), owned),
                pl.BlockSpec((1, rows, tail.shape[2]), owned),
                pl.BlockSpec((1, 2, BLOCK, BLOCK), lambda i, j, s, o, l: (level(s[2]), 0, 0, 0)),
            ],
            out_specs=pl.BlockSpec((rows, planes * plane_cells), lambda i, j, s, o, l: (0, i)),
        ),
        compiler_params=pltpu.CompilerParams(vmem_limit_bytes=40 << 20),
        cost_estimate=pl.CostEstimate(
            flops=0, bytes_accessed=4 * rows * steps * planes * plane_cells, transcendentals=0
        ),
        name="unpacked",
    )(sizes, owner, local, head, tail, spreading)


def laid_kernel(planes, steps, sizes, head, tail, out, zeros, sems):
    band_count = head.shape[0]
    per_device = sizes[0] // (planes * band_count)
    cells = planes * BOX * BOX
    zeros[...] = jnp.zeros_like(zeros)

    def place_of(unit):
        owner = jnp.minimum(unit // per_device, band_count - 1)
        return (owner, unit - owner * per_device)

    def target(unit):
        return out.at[:, pl.ds(pl.multiple_of(unit * cells, cells), cells)]

    def start(unit, carry):
        owner, place = place_of(unit)
        live = unit * planes < sizes[0]

        @pl.when(live & (place == 0))
        def _():
            source = head.at[owner, :, pl.ds(0, cells)]
            pltpu.make_async_copy(source, target(unit), sems.at[unit]).start()

        @pl.when(live & (place > 0))
        def _():
            lane = pl.multiple_of(jnp.maximum(place - 1, 0) * cells, cells)
            source = tail.at[owner, :, pl.ds(lane, cells)]
            pltpu.make_async_copy(source, target(unit), sems.at[unit]).start()

        @pl.when(unit * planes >= sizes[0])
        def _():
            pltpu.make_async_copy(zeros, target(unit), sems.at[unit]).start()

        return carry

    def finish(unit, carry):
        pltpu.make_async_copy(zeros, target(unit), sems.at[unit]).wait()
        return carry

    lax.fori_loop(0, steps, start, 0)
    lax.fori_loop(0, steps, finish, 0)


def laid_out(head, tail, sizes, steps, planes):
    rows = head.shape[1]
    cells = planes * BOX * BOX
    anywhere = pl.BlockSpec(memory_space=pl.ANY)
    return pl.pallas_call(
        functools.partial(laid_kernel, planes, steps),
        out_shape=jax.ShapeDtypeStruct((rows, steps * cells), head.dtype),
        in_specs=[pl.BlockSpec(memory_space=pltpu.SMEM), anywhere, anywhere],
        out_specs=anywhere,
        scratch_shapes=[pltpu.VMEM((rows, cells), head.dtype), pltpu.SemaphoreType.DMA((steps,))],
        cost_estimate=pl.CostEstimate(
            flops=0, bytes_accessed=4 * rows * steps * cells, transcendentals=0
        ),
        name="laid_out",
    )(sizes, head, tail)


def summed(partial_value, band_count):
    blocks = partial_value.reshape(band_count, NB // band_count, NB)
    blocks = lax.all_to_all(blocks, "band", split_axis=0, concat_axis=0, tiled=True)
    mine = jnp.sum(blocks, axis=0)
    return gathered(mine, band_count).reshape(NB, NB)


def gathered(block, band_count):
    copies = jnp.broadcast_to(block[None], (band_count,) + block.shape)
    return lax.all_to_all(copies, "band", split_axis=0, concat_axis=0, tiled=True)


def hits(position, extent):
    return position[..., None] == jnp.arange(extent)


def patched_grid(shares, box_sizes, box_offsets, patch_signs, band_count, slots, planes, parts):
    per_device = units_per_device(box_sizes[:, 0], band_count)[:, None, None, None]
    place = jnp.arange(slots)[None, None, :, None]
    unit = jnp.arange(band_count)[None, :, None, None] * per_device + place
    plane = jnp.arange(planes)[None, None, None, :]
    x = jnp.where(place < per_device, unit * planes // parts + plane, -G)
    x = x + box_offsets[:, 0][:, None, None, None]
    pair = LANES // BOX
    depth = BOX // (parts * pair)
    y = jnp.arange(depth)[None, :] * pair
    lane = jnp.arange(LANES)[None, :]
    fragments = box_sizes.shape[0]
    half = jnp.bfloat16
    cube = shares.reshape(fragments, -1, LANES)
    slabs, rows_of = [], []
    for odd in range(pair):
        z = jnp.where(lane // BOX == odd, box_offsets[:, 2][:, None] + lane % BOX, -G)
        along_z = hits(z, G).astype(half)
        wide = lax.dot_general(
            cube, along_z, (((2,), (1,)), ((0,), (0,))), preferred_element_type=half
        ).reshape(fragments, -1, depth, G)
        for part in range(parts):
            own = jnp.where(unit % parts == part, x, -G).reshape(fragments, -1)
            along_x = (hits(own, G) * patch_signs[:, None, None]).astype(half)
            slabs.append(
                lax.dot_general(
                    along_x, wide, (((1,), (1,)), ((0,), (0,))), preferred_element_type=half
                )
            )
            length = (box_sizes[:, 1] // parts)[:, None]
            row = box_offsets[:, 1][:, None] + part * length + y + odd
            rows_of.append(hits(jnp.where(y + odd < length, row, -G), G).astype(half))
    total = lax.dot_general(
        jnp.stack(rows_of, 1),
        jnp.stack(slabs, 1),
        (((0, 1, 2), (0, 1, 3)), ((), ())),
        preferred_element_type=jnp.float32,
    )
    return total.transpose(1, 0, 2)


def hartree_of(patched, table, eigen):
    precise = lax.Precision.HIGH
    spectrum = jnp.einsum("abc,ci->abi", patched, table, precision=precise)
    spectrum = jnp.einsum("abc,bi->aic", spectrum, table, precision=precise)
    spectrum = jnp.einsum("abc,ai->ibc", spectrum, table, precision=precise)
    spectrum = spectrum * (
        screening
        / (eigen[:, None, None] + eigen[None, :, None] + eigen[None, None, :] + screening)
    )
    spectrum = jnp.einsum("abc,ai->ibc", spectrum, table, precision=precise)
    spectrum = jnp.einsum("abc,bi->aic", spectrum, table, precision=precise)
    return jnp.einsum("abc,ci->abi", spectrum, table, precision=precise)


def total_of(hartree, patched):
    return hartree - local_factor * jnp.cbrt(jnp.maximum(patched, 0.0))


def widened(block, width):
    return jnp.pad(block, ((0, 0),) * (block.ndim - 1) + ((0, width - block.shape[-1]),))


def chosen(choice, branches, *operands):
    if len(branches) == 1:
        return branches[0](*operands)
    half = len(branches) // 2 if len(branches) < 4 else 1
    return lax.cond(
        choice < half,
        lambda *given: chosen(choice, branches[:half], *given),
        lambda *given: chosen(choice - half, branches[half:], *given),
        *operands,
    )


def swapped(blocks):
    return lax.all_to_all(blocks, "band", split_axis=0, concat_axis=0, tiled=True)


def body(wave_coeffs, old_potential, occupations, box_sizes, box_offsets, patch_signs):
    fragment = lax.axis_index("frag")
    band_index = lax.axis_index("band")
    band_count = lax.axis_size("band")
    planes, parts = step_plan(band_count)
    cells = BOX * BOX * BOX
    cell_volume = 1.0 / BOX**3
    sizes_here = lax.dynamic_index_in_dim(box_sizes, fragment, 0, keepdims=False)
    offsets_here = lax.dynamic_index_in_dim(box_offsets, fragment, 0, keepdims=False)
    axis = jnp.arange(BOX)
    mask = (
        (axis < sizes_here[0])[:, None, None]
        & (axis < sizes_here[1])[None, :, None]
        & (axis < sizes_here[2])[None, None, :]
    )
    owner, local = live_units(sizes_here, band_count)
    widths = class_widths(band_count)
    room = tuple(max(pair) for pair in zip(*widths))
    volume = sizes_here[0] * sizes_here[1] * sizes_here[2] * 64
    tops = jnp.array([top * BOX**3 for top in CLASSES], jnp.int32)
    choice = jnp.sum((volume <= tops).astype(jnp.int32)) - 1
    unit_cells = BOX * BOX // parts
    slots = units_per_device(BOX, band_count)
    share_sizes = jnp.stack(
        [units_per_device(sizes_here[0], band_count) * planes, sizes_here[1] // parts, sizes_here[2]]
    )
    share_owner = jnp.zeros(slots, jnp.int32)
    share_local = jnp.arange(slots, dtype=jnp.int32)

    stencil = tables_of(in_plane_stencil)
    packing = tables_of(packing_table)
    spreading = tables_of(spreading_table)

    def forward(pair):
        def branch(wave, potential):
            rows, partial_value = [], 0.0
            places = ((0, 1), (1, slots - 1))
            for (first, count), width, space in zip(places, pair, room):
                trial = packed_trial(
                    wave, potential, stencil, packing, sizes_here, first, count, width, band_count
                )
                part = swapped(trial).reshape(NB, width)
                partial_value = partial_value + lax.dot_general(
                    part, part, (((1,), (1,)), ((), ())), preferred_element_type=jnp.float32
                )
                rows.append(widened(part, space))
            return (rows[0], rows[1], partial_value)

        return branch

    head, tail, partial_value = chosen(
        choice, [forward(pair) for pair in widths], wave_coeffs[0], old_potential
    )
    gram = summed(partial_value, band_count) * cell_volume
    coeff = newton_schulz(gram)

    sent, density = [], []
    for rows, width in zip((head, tail), room):
        fresh = lax.dot_general(
            coeff, rows, (((0,), (0,)), ((), ())), preferred_element_type=jnp.float32
        )
        value = jnp.sum(occupations[0][:, None] * fresh * fresh, axis=0) / NB
        density.append(jnp.broadcast_to(value.astype(jnp.bfloat16), (1, 8, width)))
        sent.append(fresh.astype(jnp.bfloat16).reshape(band_count, NB // band_count, width))
    sent_head, sent_tail = sent
    share = unpacked(
        density[0],
        density[1],
        spreading,
        share_sizes,
        share_owner,
        share_local,
        slots,
        planes,
        1,
        unit_cells,
    )
    share = share[0].reshape(-1, LANES)
    shares = lax.all_gather(share, ("frag", "band"), axis=0, tiled=True)

    def early(pair):
        def branch(sent):
            return widened(swapped(sent[:, :, : pair[0]]), room[0])

        return branch

    back_head = lax.switch(choice, [early(pair) for pair in widths], sent_head)

    table, eigen = lax.optimization_barrier(sine_table())

    rests = sorted({rest for _, rest in widths}, reverse=True)
    rests = [rest for k, rest in enumerate(rests) if k in (0, 1, 4, 6)]
    rest_here = (units_per_device(sizes_here[0], band_count) - 1) * planes
    rest_here = rest_here * (sizes_here[1] // parts) * sizes_here[2]
    late_choice = jnp.sum((rest_here <= jnp.array(rests)).astype(jnp.int32)) - 1

    def late(rest):
        def branch(sent, shares):
            back = swapped(sent[:, :, :rest])
            patched = patched_grid(
                shares, box_sizes, box_offsets, patch_signs, band_count, slots, planes, parts
            )
            hartree = hartree_of(patched, table, eigen)

            def slab_of(grid):
                rows = G // band_count
                return lax.dynamic_slice_in_dim(grid, band_index * rows, rows)

            def window_of(grid):
                extended = jnp.pad(grid, ((0, BOX), (0, BOX), (0, BOX)))
                return lax.dynamic_slice(
                    extended, (offsets_here[0], offsets_here[1], offsets_here[2]), (BOX, BOX, BOX)
                )

            slab = total_of(slab_of(hartree), slab_of(patched))
            window = total_of(window_of(hartree), window_of(patched))
            window = jnp.where(mask, window, 0.0).reshape(1, cells)
            return (widened(back, room[1]), window, slab)

        return branch

    back_tail, window, slab = chosen(
        late_choice, [late(rest) for rest in rests], sent_tail, shares
    )
    def spread_out(head, tail):
        return unpacked(
            head,
            tail,
            spreading,
            sizes_here,
            owner,
            local,
            BOX // planes,
            planes,
            parts,
            BOX * BOX,
        )

    if parts == 1:
        waves_out = lax.cond(
            (sizes_here[1] < BOX) | (sizes_here[2] < BOX),
            spread_out,
            lambda head, tail: laid_out(head, tail, sizes_here, BOX // planes, planes),
            back_head,
            back_tail,
        )
    else:
        waves_out = spread_out(back_head, back_tail)
    return (waves_out[None], window, slab)


def solution(mesh):
    placed = (P("frag", "band", None), P("frag", None), P("frag", None), P(), P(), P())
    return jax.shard_map(
        body,
        mesh=mesh,
        in_specs=placed,
        out_specs=(P("frag", "band", None), P("frag", None), P("band", None, None)),
        check_vma=False,
    )
```

```python
import functools

import jax
import jax.numpy as jnp
import numpy as np
from jax import lax
from jax.experimental import pallas as pl
from jax.experimental.pallas import tpu as pltpu
from jax.sharding import PartitionSpec as P

NB = 256
BOX = 64
G = 128
NS_ITERS = 8


step_size = 0.1
screening = 0.5
local_factor = 0.75
epsilon = 1e-06


def sine_table():
    index = jnp.arange(G).astype(jnp.float32) + 1.0
    table = jnp.sqrt(2.0 / (G + 1)) * jnp.sin(jnp.pi * index[:, None] * index[None, :] / (G + 1))
    eigen = 2.0 - 2.0 * jnp.cos(jnp.pi * index / (G + 1))
    return (table, eigen)


def newton_schulz(gram):
    highest = lax.Precision.HIGHEST
    frobenius = jnp.sqrt(jnp.sum(gram * gram) + epsilon)
    identity = jnp.eye(NB, dtype=jnp.float32)
    square_part = gram / frobenius
    inverse_part = identity
    for sweep in range(NS_ITERS):
        newton_step = 0.5 * (
            3.0 * identity
            - jnp.dot(
                inverse_part, square_part, precision=highest, preferred_element_type=jnp.float32
            )
        )
        square_part = jnp.dot(
            square_part, newton_step, precision=highest, preferred_element_type=jnp.float32
        )
        inverse_part = jnp.dot(
            newton_step, inverse_part, precision=highest, preferred_element_type=jnp.float32
        )
    return (inverse_part / jnp.sqrt(frobenius)).astype(jnp.bfloat16)


GROUP = 8 * BOX
LANES = 128
BLOCK = 256


def step_plan(band_count):
    return (2, 1) if 16 % band_count == 0 else (1, 2)


CLASSES = (64, 48, 36, 32, 27, 18, 8)


def units_per_device(size_x, band_count):
    planes, parts = step_plan(band_count)
    return size_x * parts // (planes * band_count)


def live_units(sizes, band_count):
    planes, parts = step_plan(band_count)
    unit = jnp.arange(BOX // planes * parts, dtype=jnp.int32)
    per_device = units_per_device(sizes[0], band_count)
    owner = jnp.minimum(unit // per_device, band_count - 1)
    return (owner, unit % per_device)


def class_widths(band_count):
    planes, parts = step_plan(band_count)
    lengths = (BOX // 2, BOX * 3 // 4, BOX)
    widths = []
    for top, below in zip(CLASSES, CLASSES[1:] + (0,)):
        first, rest = 0, 0
        for x in lengths:
            for y in lengths:
                for z in lengths:
                    if below * BOX**3 < x * y * z * 64 <= top * BOX**3:
                        unit = planes * y * z // parts
                        first = max(first, unit)
                        rest = max(rest, (units_per_device(x, band_count) - 1) * unit)
        widths.append((first, rest))
    return widths


def trial_kernel(planes, parts, first_place, sizes, prev, main, after, potential, stencil, packing, out, held):
    band_count = pl.num_programs(0)
    per_device = units_per_device(sizes[0], band_count)
    index = pl.program_id(1)
    unit = pl.program_id(0) * per_device + first_place + index
    step, part = unit // parts, unit % parts
    live = first_place + index < per_device
    size_x, size_y, size_z = sizes[0], sizes[1], sizes[2]
    plane_cells = BOX * BOX
    span = plane_cells // parts
    groups = size_y // (8 * parts)
    rows, width = out.shape[1:]
    start = part * groups * GROUP if parts > 1 else 0
    live_end = size_y * BOX
    blocks = span // BLOCK

    def at(ref, first, offset, lanes):
        if parts > 1:
            offset = pl.multiple_of(start + offset, LANES)
        return ref[:, pl.ds(first + offset, lanes)]

    def chunk(p, offset):
        if parts == 1:
            if not 0 <= offset < plane_cells:
                return jnp.zeros((rows, LANES), jnp.bfloat16)
            value = main[:, pl.ds(p * plane_cells + offset, LANES)]
            if offset < span // 2:
                return value
            return jnp.where(offset < live_end, value, jnp.zeros_like(value))
        lane = start + offset
        inside = (lane >= 0) & (lane < live_end)
        lane = pl.multiple_of(jnp.clip(lane, 0, plane_cells - LANES), LANES)
        value = main[:, pl.ds(p * plane_cells + lane, LANES)]
        return jnp.where(inside, value, jnp.zeros_like(value))

    def in_plane(p):
        chunks = [chunk(p, k * LANES) for k in range(-1, span // LANES + 1)]
        windows = [jnp.concatenate(chunks[2 * b : 2 * b + 4], axis=1) for b in range(blocks)]
        return jnp.dot(stack(windows), stencil[0], preferred_element_type=jnp.float32)

    def trial_block(p, beside, b, below_on, above_on):
        plane_cells_at = p * plane_cells
        offset = b * BLOCK
        below, below_at = (prev, 0) if p == 0 else (main, plane_cells_at - plane_cells)
        above, above_at = (after, 0) if p == planes - 1 else (main, plane_cells_at + plane_cells)
        v = at(main, plane_cells_at, offset, BLOCK).astype(jnp.float32)
        total = beside[b * rows : (b + 1) * rows, :]
        total = total + below_on * at(below, below_at, offset, BLOCK).astype(jnp.float32)
        total = total + above_on * at(above, above_at, offset, BLOCK).astype(jnp.float32)
        own = (1.0 - 3.0 * step_size) - step_size * at(potential, plane_cells_at, offset, BLOCK)
        return own * v + (0.5 * step_size) * total

    def ends(p):
        x = step * planes + p
        return (jnp.where(x > 0, 1.0, 0.0), jnp.where(x + 1 < size_x, 1.0, 0.0))

    @pl.when(index == 0)
    def _():
        filled = jnp.clip(per_device - first_place, 0, pl.num_programs(1))
        filled = filled * planes * groups * (8 * size_z)

        def clear(k, carry):
            lane = pl.multiple_of(k * LANES, LANES)
            out[0, :, pl.ds(lane, LANES)] = jnp.zeros((rows, LANES), out.dtype)
            return carry

        lax.fori_loop(filled // LANES, width // LANES, clear, 0)

    depth = blocks * BLOCK // GROUP
    segments = ((0, depth // 2), (depth // 2, depth * 3 // 4), (depth * 3 // 4, depth))
    doubled = jnp.where(size_z == 32, 2, 1)

    @pl.when(live)
    def _():
        for p in range(planes):
            beside = in_plane(p)
            below_on, above_on = ends(p)
            target = (index * planes + p) * groups * (8 * size_z)
            for first, last in segments:

                @pl.when(first < groups)
                def _(first=first, last=last):
                    for b in range(first * GROUP // BLOCK, last * GROUP // BLOCK):
                        value = trial_block(p, beside, b, below_on, above_on)
                        held[:, b * BLOCK : (b + 1) * BLOCK] = value.astype(held.dtype)

            @pl.when(size_z == BOX)
            def _():
                def group_copy(group, carry):
                    lane = pl.multiple_of(target + group * GROUP, GROUP)
                    base = pl.multiple_of(group * GROUP, GROUP)
                    out[0, :, pl.ds(lane, GROUP)] = held[:, pl.ds(base, GROUP)]
                    return carry

                lax.fori_loop(0, groups, group_copy, 0)

            @pl.when(size_z < BOX)
            def _():
                for j in range(3):
                    begin = (j if j != 1 else doubled) * LANES
                    picked = []
                    for group in range(depth):
                        at_lane = begin + group * GROUP
                        if j == 1:
                            at_lane = pl.multiple_of(at_lane, LANES)
                        picked.append(held[:, pl.ds(at_lane, BLOCK)])
                    packed = jnp.dot(stack(picked), packing[0, j], preferred_element_type=jnp.float32)

                    @pl.when((size_z == 48) | (j < 2))
                    def _(j=j, packed=packed):
                        for first, last in segments:

                            @pl.when(first < groups)
                            def _(first=first, last=last):
                                for group in range(first, last):
                                    lane = target + group * (8 * size_z) + j * LANES
                                    lane = pl.multiple_of(lane, LANES)
                                    value = packed[group * rows : (group + 1) * rows, :]
                                    out[0, :, pl.ds(lane, LANES)] = value.astype(out.dtype)


def stack(pieces):
    if pieces[0].shape[0] % 16:
        pieces = [piece.astype(jnp.float32) for piece in pieces]
    return jnp.concatenate(pieces, axis=0).astype(jnp.bfloat16)


def packing_table(size_z):
    j = np.arange(3)[:, None, None]
    k = np.arange(BLOCK)[None, :, None]
    lane = j * LANES + np.arange(LANES)[None, None, :]
    begin = (2 * j if size_z == 32 else j) * LANES
    source = lane // size_z * BOX + lane % size_z - begin
    return (source == k) & (lane < 8 * size_z)


def spreading_table(size_z):
    i = np.arange(2)[:, None, None]
    k = np.arange(BLOCK)[None, :, None]
    lane = i * BLOCK + np.arange(BLOCK)[None, None, :]
    begin = (i if size_z == 48 else 0) * LANES
    source = lane // BOX * size_z + lane % BOX - begin
    return (source == k) & (lane % BOX < size_z)


def in_plane_stencil(size_z):
    source = np.arange(2 * BLOCK)[:, None] - LANES
    target = np.arange(BLOCK)[None, :]
    along_y = np.abs(source - target) == BOX
    along_z = (np.abs(source - target) == 1) & ((source + LANES) // BOX == (target + LANES) // BOX)
    return (along_y | along_z) & ((source + LANES) % BOX < size_z)


def tables_of(make):
    return jnp.asarray(np.stack([make(z) for z in (32, 48, 64)]), jnp.bfloat16)


def level(size_z):
    return size_z // 16 - 2


def packed_trial(wave, potential, stencil, packing, sizes, first_place, places, width, band_count):
    rows = wave.shape[0]
    planes, parts = step_plan(band_count)
    plane_cells = BOX * BOX

    def step(i, j, sizes):
        per_device = units_per_device(sizes[0], band_count)
        return (i * per_device + jnp.minimum(first_place + j, per_device - 1)) // parts

    def plane(shift):
        return lambda i, j, s: (0, jnp.clip(step(i, j, s) * planes + shift, 0, s[0] - 1))

    share = places * planes * plane_cells * band_count // parts
    return pl.pallas_call(
        functools.partial(trial_kernel, planes, parts, first_place),
        out_shape=jax.ShapeDtypeStruct((band_count, rows, width), jnp.bfloat16),
        grid_spec=pltpu.PrefetchScalarGridSpec(
            num_scalar_prefetch=1,
            grid=(band_count, places),
            in_specs=[
                pl.BlockSpec((rows, plane_cells), plane(-1)),
                pl.BlockSpec((rows, planes * plane_cells), lambda i, j, s: (0, step(i, j, s))),
                pl.BlockSpec((rows, plane_cells), plane(planes)),
                pl.BlockSpec((1, planes * plane_cells), lambda i, j, s: (0, step(i, j, s))),
                pl.BlockSpec((1, 2 * BLOCK, BLOCK), lambda i, j, s: (level(s[2]), 0, 0)),
                pl.BlockSpec((1, 3, BLOCK, LANES), lambda i, j, s: (level(s[2]), 0, 0, 0)),
            ],
            out_specs=pl.BlockSpec((1, rows, width), lambda i, j, s: (i, 0, 0)),
            scratch_shapes=[pltpu.VMEM((rows, plane_cells // parts), jnp.bfloat16)],
        ),
        compiler_params=pltpu.CompilerParams(vmem_limit_bytes=40 << 20),
        cost_estimate=pl.CostEstimate(
            flops=1024 * rows * share, bytes_accessed=6 * rows * share, transcendentals=0
        ),
        name="packed_trial",
    )(sizes, wave, wave, wave, potential, stencil, packing)


def unpack_kernel(planes, parts, plane_cells, sizes, owner, local, head, tail, spreading, out):
    step, part = pl.program_id(0), pl.program_id(1)
    size_x, size_y, size_z = sizes[0], sizes[1], sizes[2]
    place = local[step * parts + part]
    groups = size_y // (8 * parts)
    rows = out.shape[0]
    live = step * planes < size_x
    source = jnp.maximum(place - 1, 0) * planes * groups * (8 * size_z)

    @pl.when((part == 0) & ((size_y * BOX < plane_cells) | ~live))
    def _():
        def clear(k, carry):
            out[:, pl.ds(pl.multiple_of(k * GROUP, GROUP), GROUP)] = jnp.zeros(
                (rows, GROUP), out.dtype
            )
            return carry

        lax.fori_loop(0, planes * plane_cells // GROUP, clear, 0)

    def copy_from(packed):
        for p in range(planes):

            def group_copy(group, carry):
                base = pl.multiple_of(p * plane_cells + (part * groups + group) * GROUP, GROUP)
                at = pl.multiple_of(source + (p * groups + group) * GROUP, GROUP)
                out[:, pl.ds(base, GROUP)] = packed[0, :, pl.ds(at, GROUP)]
                return carry

            lax.fori_loop(0, groups, group_copy, 0)

    depth = plane_cells // (GROUP * parts)
    segments = ((0, depth // 2), (depth // 2, depth * 3 // 4), (depth * 3 // 4, depth))
    if depth % 4:
        segments = ((k, k + 1) for k in range(depth))

    def spread_from(packed):
        last_lane = packed.shape[2] - BLOCK
        for p in range(planes):
            for i in range(2):
                shift = jnp.where(size_z == 48, i, 0) * LANES
                picked = []
                for group in range(depth):
                    at = source + (p * groups + group) * (8 * size_z) + shift
                    at = pl.multiple_of(jnp.minimum(at, last_lane), LANES)
                    picked.append(packed[0, :, pl.ds(at, BLOCK)])
                spread = jnp.dot(stack(picked), spreading[0, i], preferred_element_type=jnp.float32)
                for first, last in segments:

                    @pl.when(first < groups)
                    def _(first=first, last=last, spread=spread, i=i, p=p):
                        for group in range(first, last):
                            lane = p * plane_cells + (part * groups + group) * GROUP + i * BLOCK
                            lane = pl.multiple_of(lane, BLOCK)
                            value = spread[group * rows : (group + 1) * rows, :]
                            out[:, pl.ds(lane, BLOCK)] = value.astype(out.dtype)

    for packed, chosen in ((head, place == 0), (tail, place > 0)):
        pl.when(live & chosen & (size_z == BOX))(functools.partial(copy_from, packed))
        pl.when(live & chosen & (size_z < BOX))(functools.partial(spread_from, packed))


def unpacked(head, tail, spreading, sizes, owner, local, steps, planes, parts, plane_cells):
    rows = head.shape[1]

    def owned(i, j, s, o, l):
        return (o[i * parts + j], 0, 0)

    return pl.pallas_call(
        functools.partial(unpack_kernel, planes, parts, plane_cells),
        out_shape=jax.ShapeDtypeStruct((rows, steps * planes * plane_cells), head.dtype),
        grid_spec=pltpu.PrefetchScalarGridSpec(
            num_scalar_prefetch=3,
            grid=(steps, parts),
            in_specs=[
                pl.BlockSpec((1, rows, head.shape[2]), owned),
                pl.BlockSpec((1, rows, tail.shape[2]), owned),
                pl.BlockSpec((1, 2, BLOCK, BLOCK), lambda i, j, s, o, l: (level(s[2]), 0, 0, 0)),
            ],
            out_specs=pl.BlockSpec((rows, planes * plane_cells), lambda i, j, s, o, l: (0, i)),
        ),
        compiler_params=pltpu.CompilerParams(vmem_limit_bytes=40 << 20),
        cost_estimate=pl.CostEstimate(
            flops=0, bytes_accessed=4 * rows * steps * planes * plane_cells, transcendentals=0
        ),
        name="unpacked",
    )(sizes, owner, local, head, tail, spreading)


def laid_kernel(planes, band_count, sizes, head, tail, out):
    unit = pl.program_id(0)
    per_device = sizes[0] // (planes * band_count)
    place = unit - jnp.minimum(unit // per_device, band_count - 1) * per_device
    live = unit * planes < sizes[0]

    @pl.when(live & (place == 0))
    def _():
        out[...] = head[0]

    @pl.when(live & (place > 0))
    def _():
        out[...] = tail[0]

    @pl.when(unit * planes >= sizes[0])
    def _():
        out[...] = jnp.zeros_like(out)


def laid_out(head, tail, sizes, steps, planes):
    band_count, rows = head.shape[:2]
    cells = planes * BOX * BOX

    def owner_of(unit, sizes):
        return jnp.minimum(unit // (sizes[0] // (planes * band_count)), band_count - 1)

    def rest_of(unit, sizes):
        per_device = sizes[0] // (planes * band_count)
        place = unit - owner_of(unit, sizes) * per_device
        return jnp.clip(place - 1, 0, per_device - 2)

    return pl.pallas_call(
        functools.partial(laid_kernel, planes, band_count),
        out_shape=jax.ShapeDtypeStruct((rows, steps * cells), head.dtype),
        grid_spec=pltpu.PrefetchScalarGridSpec(
            num_scalar_prefetch=1,
            grid=(steps,),
            in_specs=[
                pl.BlockSpec((1, rows, cells), lambda i, s: (owner_of(i, s), 0, 0)),
                pl.BlockSpec((1, rows, cells), lambda i, s: (owner_of(i, s), 0, rest_of(i, s))),
            ],
            out_specs=pl.BlockSpec((rows, cells), lambda i, s: (0, i)),
        ),
        compiler_params=pltpu.CompilerParams(vmem_limit_bytes=40 << 20),
        cost_estimate=pl.CostEstimate(
            flops=0, bytes_accessed=4 * rows * steps * cells, transcendentals=0
        ),
        name="laid_out",
    )(sizes, head, tail)


def summed(partial_value, band_count):
    blocks = partial_value.reshape(band_count, NB // band_count, NB)
    blocks = lax.all_to_all(blocks, "band", split_axis=0, concat_axis=0, tiled=True)
    mine = jnp.sum(blocks, axis=0)
    return gathered(mine, band_count).reshape(NB, NB)


def gathered(block, band_count):
    copies = jnp.broadcast_to(block[None], (band_count,) + block.shape)
    return lax.all_to_all(copies, "band", split_axis=0, concat_axis=0, tiled=True)


def hits(position, extent):
    return position[..., None] == jnp.arange(extent)


def patched_grid(shares, box_sizes, box_offsets, patch_signs, band_count, slots, planes, parts):
    per_device = units_per_device(box_sizes[:, 0], band_count)[:, None, None, None]
    place = jnp.arange(slots)[None, None, :, None]
    unit = jnp.arange(band_count)[None, :, None, None] * per_device + place
    plane = jnp.arange(planes)[None, None, None, :]
    x = jnp.where(place < per_device, unit * planes // parts + plane, -G)
    x = x + box_offsets[:, 0][:, None, None, None]
    pair = LANES // BOX
    depth = BOX // (parts * pair)
    y = jnp.arange(depth)[None, :] * pair
    lane = jnp.arange(LANES)[None, :]
    fragments = box_sizes.shape[0]
    half = jnp.bfloat16
    cube = shares.reshape(fragments, -1, LANES)
    slabs, rows_of = [], []
    for odd in range(pair):
        z = jnp.where(lane // BOX == odd, box_offsets[:, 2][:, None] + lane % BOX, -G)
        along_z = hits(z, G).astype(half)
        wide = lax.dot_general(
            cube, along_z, (((2,), (1,)), ((0,), (0,))), preferred_element_type=half
        ).reshape(fragments, -1, depth, G)
        for part in range(parts):
            own = jnp.where(unit % parts == part, x, -G).reshape(fragments, -1)
            along_x = (hits(own, G) * patch_signs[:, None, None]).astype(half)
            slabs.append(
                lax.dot_general(
                    along_x, wide, (((1,), (1,)), ((0,), (0,))), preferred_element_type=half
                )
            )
            length = (box_sizes[:, 1] // parts)[:, None]
            row = box_offsets[:, 1][:, None] + part * length + y + odd
            rows_of.append(hits(jnp.where(y + odd < length, row, -G), G).astype(half))
    total = lax.dot_general(
        jnp.stack(rows_of, 1),
        jnp.stack(slabs, 1),
        (((0, 1, 2), (0, 1, 3)), ((), ())),
        preferred_element_type=jnp.float32,
    )
    return total.transpose(1, 0, 2)


def hartree_of(patched, table, eigen):
    precise = lax.Precision.HIGH
    spectrum = jnp.einsum("abc,ci->abi", patched, table, precision=precise)
    spectrum = jnp.einsum("abc,bi->aic", spectrum, table, precision=precise)
    spectrum = jnp.einsum("abc,ai->ibc", spectrum, table, precision=precise)
    spectrum = spectrum * (
        screening
        / (eigen[:, None, None] + eigen[None, :, None] + eigen[None, None, :] + screening)
    )
    spectrum = jnp.einsum("abc,ai->ibc", spectrum, table, precision=precise)
    spectrum = jnp.einsum("abc,bi->aic", spectrum, table, precision=precise)
    return jnp.einsum("abc,ci->abi", spectrum, table, precision=precise)


def total_of(hartree, patched):
    return hartree - local_factor * jnp.cbrt(jnp.maximum(patched, 0.0))


def widened(block, width):
    return jnp.pad(block, ((0, 0),) * (block.ndim - 1) + ((0, width - block.shape[-1]),))


def chosen(choice, branches, *operands):
    if len(branches) == 1:
        return branches[0](*operands)
    half = len(branches) // 2 if len(branches) < 4 else 1
    return lax.cond(
        choice < half,
        lambda *given: chosen(choice, branches[:half], *given),
        lambda *given: chosen(choice - half, branches[half:], *given),
        *operands,
    )


def swapped(blocks):
    return lax.all_to_all(blocks, "band", split_axis=0, concat_axis=0, tiled=True)


def body(wave_coeffs, old_potential, occupations, box_sizes, box_offsets, patch_signs):
    fragment = lax.axis_index("frag")
    band_index = lax.axis_index("band")
    band_count = lax.axis_size("band")
    planes, parts = step_plan(band_count)
    cells = BOX * BOX * BOX
    cell_volume = 1.0 / BOX**3
    sizes_here = lax.dynamic_index_in_dim(box_sizes, fragment, 0, keepdims=False)
    offsets_here = lax.dynamic_index_in_dim(box_offsets, fragment, 0, keepdims=False)
    axis = jnp.arange(BOX)
    mask = (
        (axis < sizes_here[0])[:, None, None]
        & (axis < sizes_here[1])[None, :, None]
        & (axis < sizes_here[2])[None, None, :]
    )
    owner, local = live_units(sizes_here, band_count)
    widths = class_widths(band_count)
    room = tuple(max(pair) for pair in zip(*widths))
    volume = sizes_here[0] * sizes_here[1] * sizes_here[2] * 64
    tops = jnp.array([top * BOX**3 for top in CLASSES], jnp.int32)
    choice = jnp.sum((volume <= tops).astype(jnp.int32)) - 1
    unit_cells = BOX * BOX // parts
    slots = units_per_device(BOX, band_count)
    share_sizes = jnp.stack(
        [units_per_device(sizes_here[0], band_count) * planes, sizes_here[1] // parts, sizes_here[2]]
    )
    share_owner = jnp.zeros(slots, jnp.int32)
    share_local = jnp.arange(slots, dtype=jnp.int32)

    stencil = tables_of(in_plane_stencil)
    packing = tables_of(packing_table)
    spreading = tables_of(spreading_table)

    def forward(pair):
        def branch(wave, potential):
            rows, partial_value = [], 0.0
            places = ((0, 1), (1, slots - 1))
            for (first, count), width, space in zip(places, pair, room):
                trial = packed_trial(
                    wave, potential, stencil, packing, sizes_here, first, count, width, band_count
                )
                part = swapped(trial).reshape(NB, width)
                partial_value = partial_value + lax.dot_general(
                    part, part, (((1,), (1,)), ((), ())), preferred_element_type=jnp.float32
                )
                rows.append(widened(part, space))
            return (rows[0], rows[1], partial_value)

        return branch

    head, tail, partial_value = chosen(
        choice, [forward(pair) for pair in widths], wave_coeffs[0], old_potential
    )
    gram = summed(partial_value, band_count) * cell_volume
    coeff = newton_schulz(gram)

    sent, density = [], []
    for rows, width in zip((head, tail), room):
        fresh = lax.dot_general(
            coeff, rows, (((0,), (0,)), ((), ())), preferred_element_type=jnp.float32
        )
        value = jnp.sum(occupations[0][:, None] * fresh * fresh, axis=0) / NB
        density.append(jnp.broadcast_to(value.astype(jnp.bfloat16), (1, 8, width)))
        sent.append(fresh.astype(jnp.bfloat16).reshape(band_count, NB // band_count, width))
    sent_head, sent_tail = sent
    share = unpacked(
        density[0],
        density[1],
        spreading,
        share_sizes,
        share_owner,
        share_local,
        slots,
        planes,
        1,
        unit_cells,
    )
    share = share[0].reshape(-1, LANES)
    shares = lax.all_gather(share, ("frag", "band"), axis=0, tiled=True)

    def early(pair):
        def branch(sent):
            return widened(swapped(sent[:, :, : pair[0]]), room[0])

        return branch

    back_head = lax.switch(choice, [early(pair) for pair in widths], sent_head)

    table, eigen = lax.optimization_barrier(sine_table())

    rests = sorted({rest for _, rest in widths}, reverse=True)
    rests = [rest for k, rest in enumerate(rests) if k in (0, 1, 4, 6)]
    rest_here = (units_per_device(sizes_here[0], band_count) - 1) * planes
    rest_here = rest_here * (sizes_here[1] // parts) * sizes_here[2]
    late_choice = jnp.sum((rest_here <= jnp.array(rests)).astype(jnp.int32)) - 1

    def late(rest):
        def branch(sent, shares):
            back = swapped(sent[:, :, :rest])
            patched = patched_grid(
                shares, box_sizes, box_offsets, patch_signs, band_count, slots, planes, parts
            )
            hartree = hartree_of(patched, table, eigen)

            def slab_of(grid):
                rows = G // band_count
                return lax.dynamic_slice_in_dim(grid, band_index * rows, rows)

            def window_of(grid):
                extended = jnp.pad(grid, ((0, BOX), (0, BOX), (0, BOX)))
                return lax.dynamic_slice(
                    extended, (offsets_here[0], offsets_here[1], offsets_here[2]), (BOX, BOX, BOX)
                )

            slab = total_of(slab_of(hartree), slab_of(patched))
            window = total_of(window_of(hartree), window_of(patched))
            window = jnp.where(mask, window, 0.0).reshape(1, cells)
            return (widened(back, room[1]), window, slab)

        return branch

    back_tail, window, slab = chosen(
        late_choice, [late(rest) for rest in rests], sent_tail, shares
    )
    def spread_out(head, tail):
        return unpacked(
            head,
            tail,
            spreading,
            sizes_here,
            owner,
            local,
            BOX // planes,
            planes,
            parts,
            BOX * BOX,
        )

    if parts == 1:
        waves_out = lax.cond(
            (sizes_here[1] < BOX) | (sizes_here[2] < BOX),
            spread_out,
            lambda head, tail: laid_out(head, tail, sizes_here, BOX // planes, planes),
            back_head,
            back_tail,
        )
    else:
        waves_out = spread_out(back_head, back_tail)
    return (waves_out[None], window, slab)


def solution(mesh):
    placed = (P("frag", "band", None), P("frag", None), P("frag", None), P(), P(), P())
    return jax.shard_map(
        body,
        mesh=mesh,
        in_specs=placed,
        out_specs=(P("frag", "band", None), P("frag", None), P("band", None, None)),
        check_vma=False,
    )
```

```python
import functools

import jax
import jax.numpy as jnp
import numpy as np
from jax import lax
from jax.experimental import pallas as pl
from jax.experimental.pallas import tpu as pltpu
from jax.sharding import PartitionSpec as P

NB = 256
BOX = 64
G = 128
NS_ITERS = 8


step_size = 0.1
screening = 0.5
local_factor = 0.75
epsilon = 1e-06


def sine_table():
    index = jnp.arange(G).astype(jnp.float32) + 1.0
    table = jnp.sqrt(2.0 / (G + 1)) * jnp.sin(jnp.pi * index[:, None] * index[None, :] / (G + 1))
    eigen = 2.0 - 2.0 * jnp.cos(jnp.pi * index / (G + 1))
    return (table, eigen)


def newton_schulz(gram):
    highest = lax.Precision.HIGHEST
    frobenius = jnp.sqrt(jnp.sum(gram * gram) + epsilon)
    identity = jnp.eye(NB, dtype=jnp.float32)
    square_part = gram / frobenius
    inverse_part = identity
    for sweep in range(NS_ITERS):
        newton_step = 0.5 * (
            3.0 * identity
            - jnp.dot(
                inverse_part, square_part, precision=highest, preferred_element_type=jnp.float32
            )
        )
        square_part = jnp.dot(
            square_part, newton_step, precision=highest, preferred_element_type=jnp.float32
        )
        inverse_part = jnp.dot(
            newton_step, inverse_part, precision=highest, preferred_element_type=jnp.float32
        )
    return (inverse_part / jnp.sqrt(frobenius)).astype(jnp.bfloat16)


GROUP = 8 * BOX
LANES = 128
BLOCK = 256


def step_plan(band_count):
    return (2, 1) if 16 % band_count == 0 else (1, 2)


CLASSES = (64, 48, 36, 32, 27, 18, 8)


def units_per_device(size_x, band_count):
    planes, parts = step_plan(band_count)
    return size_x * parts // (planes * band_count)


def live_units(sizes, band_count):
    planes, parts = step_plan(band_count)
    unit = jnp.arange(BOX // planes * parts, dtype=jnp.int32)
    per_device = units_per_device(sizes[0], band_count)
    owner = jnp.minimum(unit // per_device, band_count - 1)
    return (owner, unit % per_device)


def class_widths(band_count):
    planes, parts = step_plan(band_count)
    lengths = (BOX // 2, BOX * 3 // 4, BOX)
    widths = []
    for top, below in zip(CLASSES, CLASSES[1:] + (0,)):
        first, rest = 0, 0
        for x in lengths:
            for y in lengths:
                for z in lengths:
                    if below * BOX**3 < x * y * z * 64 <= top * BOX**3:
                        unit = planes * y * z // parts
                        first = max(first, unit)
                        rest = max(rest, (units_per_device(x, band_count) - 1) * unit)
        widths.append((first, rest))
    return widths


def trial_kernel(planes, parts, first_place, sizes, prev, main, after, potential, stencil, packing, out, held):
    band_count = pl.num_programs(0)
    per_device = units_per_device(sizes[0], band_count)
    index = pl.program_id(1)
    unit = pl.program_id(0) * per_device + first_place + index
    step, part = unit // parts, unit % parts
    live = first_place + index < per_device
    size_x, size_y, size_z = sizes[0], sizes[1], sizes[2]
    plane_cells = BOX * BOX
    span = plane_cells // parts
    groups = size_y // (8 * parts)
    rows, width = out.shape[1:]
    start = part * groups * GROUP if parts > 1 else 0
    live_end = size_y * BOX
    blocks = span // BLOCK

    def at(ref, first, offset, lanes):
        if parts > 1:
            offset = pl.multiple_of(start + offset, LANES)
        return ref[:, pl.ds(first + offset, lanes)]

    def chunk(p, offset):
        if parts == 1:
            if not 0 <= offset < plane_cells:
                return jnp.zeros((rows, LANES), jnp.bfloat16)
            value = main[:, pl.ds(p * plane_cells + offset, LANES)]
            if offset < span // 2:
                return value
            return jnp.where(offset < live_end, value, jnp.zeros_like(value))
        lane = start + offset
        inside = (lane >= 0) & (lane < live_end)
        lane = pl.multiple_of(jnp.clip(lane, 0, plane_cells - LANES), LANES)
        value = main[:, pl.ds(p * plane_cells + lane, LANES)]
        return jnp.where(inside, value, jnp.zeros_like(value))

    def in_plane(p):
        chunks = [chunk(p, k * LANES) for k in range(-1, span // LANES + 1)]
        windows = [jnp.concatenate(chunks[2 * b : 2 * b + 4], axis=1) for b in range(blocks)]
        return jnp.dot(stack(windows), stencil[0], preferred_element_type=jnp.float32)

    def trial_block(p, beside, b, below_on, above_on):
        plane_cells_at = p * plane_cells
        offset = b * BLOCK
        below, below_at = (prev, 0) if p == 0 else (main, plane_cells_at - plane_cells)
        above, above_at = (after, 0) if p == planes - 1 else (main, plane_cells_at + plane_cells)
        v = at(main, plane_cells_at, offset, BLOCK).astype(jnp.float32)
        total = beside[b * rows : (b + 1) * rows, :]
        total = total + below_on * at(below, below_at, offset, BLOCK).astype(jnp.float32)
        total = total + above_on * at(above, above_at, offset, BLOCK).astype(jnp.float32)
        own = (1.0 - 3.0 * step_size) - step_size * at(potential, plane_cells_at, offset, BLOCK)
        return own * v + (0.5 * step_size) * total

    def ends(p):
        x = step * planes + p
        return (jnp.where(x > 0, 1.0, 0.0), jnp.where(x + 1 < size_x, 1.0, 0.0))

    @pl.when(index == 0)
    def _():
        filled = jnp.clip(per_device - first_place, 0, pl.num_programs(1))
        filled = filled * planes * groups * (8 * size_z)

        def clear(k, carry):
            lane = pl.multiple_of(k * LANES, LANES)
            out[0, :, pl.ds(lane, LANES)] = jnp.zeros((rows, LANES), out.dtype)
            return carry

        lax.fori_loop(filled // LANES, width // LANES, clear, 0)

    depth = blocks * BLOCK // GROUP
    segments = ((0, depth // 2), (depth // 2, depth * 3 // 4), (depth * 3 // 4, depth))
    doubled = jnp.where(size_z == 32, 2, 1)

    @pl.when(live)
    def _():
        for p in range(planes):
            beside = in_plane(p)
            below_on, above_on = ends(p)
            target = (index * planes + p) * groups * (8 * size_z)
            for first, last in segments:

                @pl.when(first < groups)
                def _(first=first, last=last):
                    for b in range(first * GROUP // BLOCK, last * GROUP // BLOCK):
                        value = trial_block(p, beside, b, below_on, above_on)
                        held[:, b * BLOCK : (b + 1) * BLOCK] = value.astype(held.dtype)

            @pl.when(size_z == BOX)
            def _():
                def group_copy(group, carry):
                    lane = pl.multiple_of(target + group * GROUP, GROUP)
                    base = pl.multiple_of(group * GROUP, GROUP)
                    out[0, :, pl.ds(lane, GROUP)] = held[:, pl.ds(base, GROUP)]
                    return carry

                lax.fori_loop(0, groups, group_copy, 0)

            @pl.when(size_z < BOX)
            def _():
                for j in range(3):
                    begin = (j if j != 1 else doubled) * LANES
                    picked = []
                    for group in range(depth):
                        at_lane = begin + group * GROUP
                        if j == 1:
                            at_lane = pl.multiple_of(at_lane, LANES)
                        picked.append(held[:, pl.ds(at_lane, BLOCK)])
                    packed = jnp.dot(stack(picked), packing[0, j], preferred_element_type=jnp.float32)

                    @pl.when((size_z == 48) | (j < 2))
                    def _(j=j, packed=packed):
                        for first, last in segments:

                            @pl.when(first < groups)
                            def _(first=first, last=last):
                                for group in range(first, last):
                                    lane = target + group * (8 * size_z) + j * LANES
                                    lane = pl.multiple_of(lane, LANES)
                                    value = packed[group * rows : (group + 1) * rows, :]
                                    out[0, :, pl.ds(lane, LANES)] = value.astype(out.dtype)


def stack(pieces):
    if pieces[0].shape[0] % 16:
        pieces = [piece.astype(jnp.float32) for piece in pieces]
    return jnp.concatenate(pieces, axis=0).astype(jnp.bfloat16)


def packing_table(size_z):
    j = np.arange(3)[:, None, None]
    k = np.arange(BLOCK)[None, :, None]
    lane = j * LANES + np.arange(LANES)[None, None, :]
    begin = (2 * j if size_z == 32 else j) * LANES
    source = lane // size_z * BOX + lane % size_z - begin
    return (source == k) & (lane < 8 * size_z)


def spreading_table(size_z):
    i = np.arange(2)[:, None, None]
    k = np.arange(BLOCK)[None, :, None]
    lane = i * BLOCK + np.arange(BLOCK)[None, None, :]
    begin = (i if size_z == 48 else 0) * LANES
    source = lane // BOX * size_z + lane % BOX - begin
    return (source == k) & (lane % BOX < size_z)


def in_plane_stencil(size_z):
    source = np.arange(2 * BLOCK)[:, None] - LANES
    target = np.arange(BLOCK)[None, :]
    along_y = np.abs(source - target) == BOX
    along_z = (np.abs(source - target) == 1) & ((source + LANES) // BOX == (target + LANES) // BOX)
    return (along_y | along_z) & ((source + LANES) % BOX < size_z)


def tables_of(make):
    return jnp.asarray(np.stack([make(z) for z in (32, 48, 64)]), jnp.bfloat16)


def level(size_z):
    return size_z // 16 - 2


def packed_trial(wave, potential, stencil, packing, sizes, first_place, places, width, band_count):
    rows = wave.shape[0]
    planes, parts = step_plan(band_count)
    plane_cells = BOX * BOX

    def step(i, j, sizes):
        per_device = units_per_device(sizes[0], band_count)
        return (i * per_device + jnp.minimum(first_place + j, per_device - 1)) // parts

    def plane(shift):
        return lambda i, j, s: (0, jnp.clip(step(i, j, s) * planes + shift, 0, s[0] - 1))

    share = places * planes * plane_cells * band_count // parts
    return pl.pallas_call(
        functools.partial(trial_kernel, planes, parts, first_place),
        out_shape=jax.ShapeDtypeStruct((band_count, rows, width), jnp.bfloat16),
        grid_spec=pltpu.PrefetchScalarGridSpec(
            num_scalar_prefetch=1,
            grid=(band_count, places),
            in_specs=[
                pl.BlockSpec((rows, plane_cells), plane(-1)),
                pl.BlockSpec((rows, planes * plane_cells), lambda i, j, s: (0, step(i, j, s))),
                pl.BlockSpec((rows, plane_cells), plane(planes)),
                pl.BlockSpec((1, planes * plane_cells), lambda i, j, s: (0, step(i, j, s))),
                pl.BlockSpec((1, 2 * BLOCK, BLOCK), lambda i, j, s: (level(s[2]), 0, 0)),
                pl.BlockSpec((1, 3, BLOCK, LANES), lambda i, j, s: (level(s[2]), 0, 0, 0)),
            ],
            out_specs=pl.BlockSpec((1, rows, width), lambda i, j, s: (i, 0, 0)),
            scratch_shapes=[pltpu.VMEM((rows, plane_cells // parts), jnp.bfloat16)],
        ),
        compiler_params=pltpu.CompilerParams(vmem_limit_bytes=40 << 20),
        cost_estimate=pl.CostEstimate(
            flops=1024 * rows * share, bytes_accessed=6 * rows * share, transcendentals=0
        ),
        name="packed_trial",
    )(sizes, wave, wave, wave, potential, stencil, packing)


def unpack_kernel(planes, parts, plane_cells, sizes, owner, local, head, tail, spreading, out):
    step, part = pl.program_id(0), pl.program_id(1)
    size_x, size_y, size_z = sizes[0], sizes[1], sizes[2]
    place = local[step * parts + part]
    groups = size_y // (8 * parts)
    rows = out.shape[0]
    live = step * planes < size_x
    source = jnp.maximum(place - 1, 0) * planes * groups * (8 * size_z)

    @pl.when((part == 0) & ((size_y * BOX < plane_cells) | ~live))
    def _():
        def clear(k, carry):
            out[:, pl.ds(pl.multiple_of(k * GROUP, GROUP), GROUP)] = jnp.zeros(
                (rows, GROUP), out.dtype
            )
            return carry

        lax.fori_loop(0, planes * plane_cells // GROUP, clear, 0)

    def copy_from(packed):
        for p in range(planes):

            def group_copy(group, carry):
                base = pl.multiple_of(p * plane_cells + (part * groups + group) * GROUP, GROUP)
                at = pl.multiple_of(source + (p * groups + group) * GROUP, GROUP)
                out[:, pl.ds(base, GROUP)] = packed[0, :, pl.ds(at, GROUP)]
                return carry

            lax.fori_loop(0, groups, group_copy, 0)

    depth = plane_cells // (GROUP * parts)
    segments = ((0, depth // 2), (depth // 2, depth * 3 // 4), (depth * 3 // 4, depth))
    if depth % 4:
        segments = ((k, k + 1) for k in range(depth))

    def spread_from(packed):
        last_lane = packed.shape[2] - BLOCK
        for p in range(planes):
            for i in range(2):
                shift = jnp.where(size_z == 48, i, 0) * LANES
                picked = []
                for group in range(depth):
                    at = source + (p * groups + group) * (8 * size_z) + shift
                    at = pl.multiple_of(jnp.minimum(at, last_lane), LANES)
                    picked.append(packed[0, :, pl.ds(at, BLOCK)])
                spread = jnp.dot(stack(picked), spreading[0, i], preferred_element_type=jnp.float32)
                for first, last in segments:

                    @pl.when(first < groups)
                    def _(first=first, last=last, spread=spread, i=i, p=p):
                        for group in range(first, last):
                            lane = p * plane_cells + (part * groups + group) * GROUP + i * BLOCK
                            lane = pl.multiple_of(lane, BLOCK)
                            value = spread[group * rows : (group + 1) * rows, :]
                            out[:, pl.ds(lane, BLOCK)] = value.astype(out.dtype)

    for packed, chosen in ((head, place == 0), (tail, place > 0)):
        pl.when(live & chosen & (size_z == BOX))(functools.partial(copy_from, packed))
        pl.when(live & chosen & (size_z < BOX))(functools.partial(spread_from, packed))


def unpacked(head, tail, spreading, sizes, owner, local, steps, planes, parts, plane_cells):
    rows = head.shape[1]

    def owned(i, j, s, o, l):
        return (o[i * parts + j], 0, 0)

    return pl.pallas_call(
        functools.partial(unpack_kernel, planes, parts, plane_cells),
        out_shape=jax.ShapeDtypeStruct((rows, steps * planes * plane_cells), head.dtype),
        grid_spec=pltpu.PrefetchScalarGridSpec(
            num_scalar_prefetch=3,
            grid=(steps, parts),
            in_specs=[
                pl.BlockSpec((1, rows, head.shape[2]), owned),
                pl.BlockSpec((1, rows, tail.shape[2]), owned),
                pl.BlockSpec((1, 2, BLOCK, BLOCK), lambda i, j, s, o, l: (level(s[2]), 0, 0, 0)),
            ],
            out_specs=pl.BlockSpec((rows, planes * plane_cells), lambda i, j, s, o, l: (0, i)),
        ),
        compiler_params=pltpu.CompilerParams(vmem_limit_bytes=40 << 20),
        cost_estimate=pl.CostEstimate(
            flops=0, bytes_accessed=4 * rows * steps * planes * plane_cells, transcendentals=0
        ),
        name="unpacked",
    )(sizes, owner, local, head, tail, spreading)


def laid_kernel(planes, band_count, sizes, head, tail, out):
    unit = pl.program_id(0)
    per_device = sizes[0] // (planes * band_count)
    place = unit - jnp.minimum(unit // per_device, band_count - 1) * per_device
    live = unit * planes < sizes[0]

    @pl.when(live & (place == 0))
    def _():
        out[...] = head[0]

    @pl.when(live & (place > 0))
    def _():
        out[...] = tail[0]

    @pl.when(unit * planes >= sizes[0])
    def _():
        out[...] = jnp.zeros_like(out)


def laid_out(head, tail, sizes, steps, planes):
    band_count, rows = head.shape[:2]
    cells = planes * BOX * BOX

    def owner_of(unit, sizes):
        return jnp.minimum(unit // (sizes[0] // (planes * band_count)), band_count - 1)

    def rest_of(unit, sizes):
        per_device = sizes[0] // (planes * band_count)
        place = unit - owner_of(unit, sizes) * per_device
        return jnp.clip(place - 1, 0, per_device - 2)

    return pl.pallas_call(
        functools.partial(laid_kernel, planes, band_count),
        out_shape=jax.ShapeDtypeStruct((rows, steps * cells), head.dtype),
        grid_spec=pltpu.PrefetchScalarGridSpec(
            num_scalar_prefetch=1,
            grid=(steps,),
            in_specs=[
                pl.BlockSpec((1, rows, cells), lambda i, s: (owner_of(i, s), 0, 0)),
                pl.BlockSpec((1, rows, cells), lambda i, s: (owner_of(i, s), 0, rest_of(i, s))),
            ],
            out_specs=pl.BlockSpec((rows, cells), lambda i, s: (0, i)),
        ),
        compiler_params=pltpu.CompilerParams(vmem_limit_bytes=40 << 20),
        cost_estimate=pl.CostEstimate(
            flops=0, bytes_accessed=4 * rows * steps * cells, transcendentals=0
        ),
        name="laid_out",
    )(sizes, head, tail)


def gram_kernel(count, scale, partial_value, out, landing, whole, sent, landed, shared, spread):
    me = lax.axis_index("band")
    rows = NB // count
    steps = range(1, count)

    def peer(step):
        return {"band": lax.rem(me + step, count)}

    def block(owner):
        return pl.ds(pl.multiple_of(owner * rows, 8), rows)

    barrier = pltpu.get_barrier_semaphore()
    for step in steps:
        pl.semaphore_signal(
            barrier, inc=1, device_id=peer(step), device_id_type=pl.DeviceIdType.MESH
        )
    pl.semaphore_wait(barrier, count - 1)
    out_copies = []
    for step in steps:
        copy = pltpu.make_async_remote_copy(
            src_ref=partial_value.at[block(lax.rem(me + step, count)), :],
            dst_ref=landing.at[step - 1],
            send_sem=sent.at[step - 1],
            recv_sem=landed.at[step - 1],
            device_id=peer(step),
            device_id_type=pl.DeviceIdType.MESH,
        )
        copy.start()
        out_copies.append(copy)
    total = partial_value[block(me), :]
    for step in steps:
        out_copies[step - 1].wait_recv()
        total = total + landing[step - 1]
    whole[block(me), :] = total * scale
    back_copies = []
    for step in steps:
        copy = pltpu.make_async_remote_copy(
            src_ref=whole.at[block(me), :],
            dst_ref=whole.at[block(me), :],
            send_sem=shared.at[step - 1],
            recv_sem=spread.at[step - 1],
            device_id=peer(step),
            device_id_type=pl.DeviceIdType.MESH,
        )
        copy.start()
        back_copies.append(copy)
    for copy in back_copies:
        copy.wait_recv()
    for copy in out_copies + back_copies:
        copy.wait_send()
    out[...] = whole[...]


def summed(partial_value, band_count, scale):
    rows = NB // band_count
    sems = pltpu.SemaphoreType.DMA((band_count - 1,))
    return pl.pallas_call(
        functools.partial(gram_kernel, band_count, scale),
        out_shape=jax.ShapeDtypeStruct((NB, NB), jnp.float32),
        in_specs=[pl.BlockSpec(memory_space=pltpu.VMEM)],
        out_specs=pl.BlockSpec(memory_space=pltpu.VMEM),
        scratch_shapes=[
            pltpu.VMEM((band_count - 1, rows, NB), jnp.float32),
            pltpu.VMEM((NB, NB), jnp.float32),
            sems,
            sems,
            sems,
            sems,
        ],
        compiler_params=pltpu.CompilerParams(collective_id=0, has_side_effects=True),
        name="gram_sum",
    )(partial_value)


def hits(position, extent):
    return position[..., None] == jnp.arange(extent)


def patched_grid(shares, box_sizes, box_offsets, patch_signs, band_count, slots, planes, parts):
    per_device = units_per_device(box_sizes[:, 0], band_count)[:, None, None, None]
    place = jnp.arange(slots)[None, None, :, None]
    unit = jnp.arange(band_count)[None, :, None, None] * per_device + place
    plane = jnp.arange(planes)[None, None, None, :]
    x = jnp.where(place < per_device, unit * planes // parts + plane, -G)
    x = x + box_offsets[:, 0][:, None, None, None]
    pair = LANES // BOX
    depth = BOX // (parts * pair)
    y = jnp.arange(depth)[None, :] * pair
    lane = jnp.arange(LANES)[None, :]
    fragments = box_sizes.shape[0]
    half = jnp.bfloat16
    cube = shares.reshape(fragments, -1, LANES)
    slabs, rows_of = [], []
    for odd in range(pair):
        z = jnp.where(lane // BOX == odd, box_offsets[:, 2][:, None] + lane % BOX, -G)
        along_z = hits(z, G).astype(half)
        wide = lax.dot_general(
            cube, along_z, (((2,), (1,)), ((0,), (0,))), preferred_element_type=half
        ).reshape(fragments, -1, depth, G)
        for part in range(parts):
            own = jnp.where(unit % parts == part, x, -G).reshape(fragments, -1)
            along_x = (hits(own, G) * patch_signs[:, None, None]).astype(half)
            slabs.append(
                lax.dot_general(
                    along_x, wide, (((1,), (1,)), ((0,), (0,))), preferred_element_type=half
                )
            )
            length = (box_sizes[:, 1] // parts)[:, None]
            row = box_offsets[:, 1][:, None] + part * length + y + odd
            rows_of.append(hits(jnp.where(y + odd < length, row, -G), G).astype(half))
    total = lax.dot_general(
        jnp.stack(rows_of, 1),
        jnp.stack(slabs, 1),
        (((0, 1, 2), (0, 1, 3)), ((), ())),
        preferred_element_type=jnp.float32,
    )
    return total.transpose(1, 0, 2)


def hartree_of(patched, table, eigen):
    precise = lax.Precision.HIGH
    spectrum = jnp.einsum("abc,ci->abi", patched, table, precision=precise)
    spectrum = jnp.einsum("abc,bi->aic", spectrum, table, precision=precise)
    spectrum = jnp.einsum("abc,ai->ibc", spectrum, table, precision=precise)
    spectrum = spectrum * (
        screening
        / (eigen[:, None, None] + eigen[None, :, None] + eigen[None, None, :] + screening)
    )
    spectrum = jnp.einsum("abc,ai->ibc", spectrum, table, precision=precise)
    spectrum = jnp.einsum("abc,bi->aic", spectrum, table, precision=precise)
    return jnp.einsum("abc,ci->abi", spectrum, table, precision=precise)


def total_of(hartree, patched):
    return hartree - local_factor * jnp.cbrt(jnp.maximum(patched, 0.0))


def widened(block, width):
    return jnp.pad(block, ((0, 0),) * (block.ndim - 1) + ((0, width - block.shape[-1]),))


def chosen(choice, branches, *operands):
    if len(branches) == 1:
        return branches[0](*operands)
    half = len(branches) // 2 if len(branches) < 4 else 1
    return lax.cond(
        choice < half,
        lambda *given: chosen(choice, branches[:half], *given),
        lambda *given: chosen(choice - half, branches[half:], *given),
        *operands,
    )


def swapped(blocks):
    return lax.all_to_all(blocks, "band", split_axis=0, concat_axis=0, tiled=True)


def body(wave_coeffs, old_potential, occupations, box_sizes, box_offsets, patch_signs):
    fragment = lax.axis_index("frag")
    band_index = lax.axis_index("band")
    band_count = lax.axis_size("band")
    planes, parts = step_plan(band_count)
    cells = BOX * BOX * BOX
    cell_volume = 1.0 / BOX**3
    sizes_here = lax.dynamic_index_in_dim(box_sizes, fragment, 0, keepdims=False)
    offsets_here = lax.dynamic_index_in_dim(box_offsets, fragment, 0, keepdims=False)
    axis = jnp.arange(BOX)
    mask = (
        (axis < sizes_here[0])[:, None, None]
        & (axis < sizes_here[1])[None, :, None]
        & (axis < sizes_here[2])[None, None, :]
    )
    owner, local = live_units(sizes_here, band_count)
    widths = class_widths(band_count)
    room = tuple(max(pair) for pair in zip(*widths))
    volume = sizes_here[0] * sizes_here[1] * sizes_here[2] * 64
    tops = jnp.array([top * BOX**3 for top in CLASSES], jnp.int32)
    choice = jnp.sum((volume <= tops).astype(jnp.int32)) - 1
    unit_cells = BOX * BOX // parts
    slots = units_per_device(BOX, band_count)
    share_sizes = jnp.stack(
        [units_per_device(sizes_here[0], band_count) * planes, sizes_here[1] // parts, sizes_here[2]]
    )
    share_owner = jnp.zeros(slots, jnp.int32)
    share_local = jnp.arange(slots, dtype=jnp.int32)

    stencil = tables_of(in_plane_stencil)
    packing = tables_of(packing_table)
    spreading = tables_of(spreading_table)

    def forward(pair):
        def branch(wave, potential):
            rows, partial_value = [], 0.0
            places = ((0, 1), (1, slots - 1))
            for (first, count), width, space in zip(places, pair, room):
                trial = packed_trial(
                    wave, potential, stencil, packing, sizes_here, first, count, width, band_count
                )
                part = swapped(trial).reshape(NB, width)
                partial_value = partial_value + lax.dot_general(
                    part, part, (((1,), (1,)), ((), ())), preferred_element_type=jnp.float32
                )
                rows.append(widened(part, space))
            return (rows[0], rows[1], partial_value)

        return branch

    head, tail, partial_value = chosen(
        choice, [forward(pair) for pair in widths], wave_coeffs[0], old_potential
    )
    gram = summed(partial_value, band_count, cell_volume)
    coeff = newton_schulz(gram)

    sent, density = [], []
    for rows, width in zip((head, tail), room):
        fresh = lax.dot_general(
            coeff, rows, (((0,), (0,)), ((), ())), preferred_element_type=jnp.float32
        )
        value = jnp.sum(occupations[0][:, None] * fresh * fresh, axis=0) / NB
        density.append(jnp.broadcast_to(value.astype(jnp.bfloat16), (1, 8, width)))
        sent.append(fresh.astype(jnp.bfloat16).reshape(band_count, NB // band_count, width))
    sent_head, sent_tail = sent
    share = unpacked(
        density[0],
        density[1],
        spreading,
        share_sizes,
        share_owner,
        share_local,
        slots,
        planes,
        1,
        unit_cells,
    )
    share = share[0].reshape(-1, LANES)
    shares = lax.all_gather(share, ("frag", "band"), axis=0, tiled=True)

    def early(pair):
        def branch(sent):
            return widened(swapped(sent[:, :, : pair[0]]), room[0])

        return branch

    back_head = lax.switch(choice, [early(pair) for pair in widths], sent_head)

    table, eigen = lax.optimization_barrier(sine_table())

    rests = sorted({rest for _, rest in widths}, reverse=True)
    rests = [rest for k, rest in enumerate(rests) if k in (0, 1, 2, 4, 6)]
    rest_here = (units_per_device(sizes_here[0], band_count) - 1) * planes
    rest_here = rest_here * (sizes_here[1] // parts) * sizes_here[2]
    late_choice = jnp.sum((rest_here <= jnp.array(rests)).astype(jnp.int32)) - 1

    def late(rest):
        def branch(sent, shares):
            back = swapped(sent[:, :, :rest])
            patched = patched_grid(
                shares, box_sizes, box_offsets, patch_signs, band_count, slots, planes, parts
            )
            hartree = hartree_of(patched, table, eigen)

            def slab_of(grid):
                rows = G // band_count
                return lax.dynamic_slice_in_dim(grid, band_index * rows, rows)

            def window_of(grid):
                extended = jnp.pad(grid, ((0, BOX), (0, BOX), (0, BOX)))
                return lax.dynamic_slice(
                    extended, (offsets_here[0], offsets_here[1], offsets_here[2]), (BOX, BOX, BOX)
                )

            slab = total_of(slab_of(hartree), slab_of(patched))
            window = total_of(window_of(hartree), window_of(patched))
            window = jnp.where(mask, window, 0.0).reshape(1, cells)
            return (widened(back, room[1]), window, slab)

        return branch

    back_tail, window, slab = chosen(
        late_choice, [late(rest) for rest in rests], sent_tail, shares
    )
    def spread_out(head, tail):
        return unpacked(
            head,
            tail,
            spreading,
            sizes_here,
            owner,
            local,
            BOX // planes,
            planes,
            parts,
            BOX * BOX,
        )

    if parts == 1:
        waves_out = lax.cond(
            (sizes_here[1] < BOX) | (sizes_here[2] < BOX),
            spread_out,
            lambda head, tail: laid_out(head, tail, sizes_here, BOX // planes, planes),
            back_head,
            back_tail,
        )
    else:
        waves_out = spread_out(back_head, back_tail)
    return (waves_out[None], window, slab)


def solution(mesh):
    placed = (P("frag", "band", None), P("frag", None), P("frag", None), P(), P(), P())
    return jax.shard_map(
        body,
        mesh=mesh,
        in_specs=placed,
        out_specs=(P("frag", "band", None), P("frag", None), P("band", None, None)),
        check_vma=False,
    )
```

```python
import functools

import jax
import jax.numpy as jnp
import numpy as np
from jax import lax
from jax.experimental import pallas as pl
from jax.experimental.pallas import tpu as pltpu
from jax.sharding import PartitionSpec as P

NB = 256
BOX = 64
G = 128
NS_ITERS = 8


step_size = 0.1
screening = 0.5
local_factor = 0.75
epsilon = 1e-06


def sine_table():
    index = jnp.arange(G).astype(jnp.float32) + 1.0
    table = jnp.sqrt(2.0 / (G + 1)) * jnp.sin(jnp.pi * index[:, None] * index[None, :] / (G + 1))
    eigen = 2.0 - 2.0 * jnp.cos(jnp.pi * index / (G + 1))
    return (table, eigen)


def newton_schulz(gram):
    highest = lax.Precision.HIGHEST
    frobenius = jnp.sqrt(jnp.sum(gram * gram) + epsilon)
    identity = jnp.eye(NB, dtype=jnp.float32)
    square_part = gram / frobenius
    inverse_part = identity
    for sweep in range(NS_ITERS):
        newton_step = 0.5 * (
            3.0 * identity
            - jnp.dot(
                inverse_part, square_part, precision=highest, preferred_element_type=jnp.float32
            )
        )
        square_part = jnp.dot(
            square_part, newton_step, precision=highest, preferred_element_type=jnp.float32
        )
        inverse_part = jnp.dot(
            newton_step, inverse_part, precision=highest, preferred_element_type=jnp.float32
        )
    return (inverse_part / jnp.sqrt(frobenius)).astype(jnp.bfloat16)


GROUP = 8 * BOX
LANES = 128
BLOCK = 256


def step_plan(band_count):
    return (2, 1) if 16 % band_count == 0 else (1, 2)


CLASSES = (64, 48, 36, 32, 27, 18, 8)


def units_per_device(size_x, band_count):
    planes, parts = step_plan(band_count)
    return size_x * parts // (planes * band_count)


def live_units(sizes, band_count):
    planes, parts = step_plan(band_count)
    unit = jnp.arange(BOX // planes * parts, dtype=jnp.int32)
    per_device = units_per_device(sizes[0], band_count)
    owner = jnp.minimum(unit // per_device, band_count - 1)
    return (owner, unit % per_device)


def class_widths(band_count):
    planes, parts = step_plan(band_count)
    lengths = (BOX // 2, BOX * 3 // 4, BOX)
    widths = []
    for top, below in zip(CLASSES, CLASSES[1:] + (0,)):
        first, rest = 0, 0
        for x in lengths:
            for y in lengths:
                for z in lengths:
                    if below * BOX**3 < x * y * z * 64 <= top * BOX**3:
                        unit = planes * y * z // parts
                        first = max(first, unit)
                        rest = max(rest, (units_per_device(x, band_count) - 1) * unit)
        widths.append((first, rest))
    return widths


def trial_kernel(planes, parts, first_place, sizes, prev, main, after, potential, stencil, packing, out, held):
    band_count = pl.num_programs(0)
    per_device = units_per_device(sizes[0], band_count)
    index = pl.program_id(1)
    unit = pl.program_id(0) * per_device + first_place + index
    step, part = unit // parts, unit % parts
    live = first_place + index < per_device
    size_x, size_y, size_z = sizes[0], sizes[1], sizes[2]
    plane_cells = BOX * BOX
    span = plane_cells // parts
    groups = size_y // (8 * parts)
    rows, width = out.shape[1:]
    start = part * groups * GROUP if parts > 1 else 0
    live_end = size_y * BOX
    blocks = span // BLOCK

    def at(ref, first, offset, lanes):
        if parts > 1:
            offset = pl.multiple_of(start + offset, LANES)
        return ref[:, pl.ds(first + offset, lanes)]

    def chunk(p, offset):
        if parts == 1:
            if not 0 <= offset < plane_cells:
                return jnp.zeros((rows, LANES), jnp.bfloat16)
            value = main[:, pl.ds(p * plane_cells + offset, LANES)]
            if offset < span // 2:
                return value
            return jnp.where(offset < live_end, value, jnp.zeros_like(value))
        lane = start + offset
        inside = (lane >= 0) & (lane < live_end)
        lane = pl.multiple_of(jnp.clip(lane, 0, plane_cells - LANES), LANES)
        value = main[:, pl.ds(p * plane_cells + lane, LANES)]
        return jnp.where(inside, value, jnp.zeros_like(value))

    def in_plane(p):
        chunks = [chunk(p, k * LANES) for k in range(-1, span // LANES + 1)]
        windows = [jnp.concatenate(chunks[2 * b : 2 * b + 4], axis=1) for b in range(blocks)]
        return jnp.dot(stack(windows), stencil[0], preferred_element_type=jnp.float32)

    def trial_block(p, beside, b, below_on, above_on):
        plane_cells_at = p * plane_cells
        offset = b * BLOCK
        below, below_at = (prev, 0) if p == 0 else (main, plane_cells_at - plane_cells)
        above, above_at = (after, 0) if p == planes - 1 else (main, plane_cells_at + plane_cells)
        v = at(main, plane_cells_at, offset, BLOCK).astype(jnp.float32)
        total = beside[b * rows : (b + 1) * rows, :]
        total = total + below_on * at(below, below_at, offset, BLOCK).astype(jnp.float32)
        total = total + above_on * at(above, above_at, offset, BLOCK).astype(jnp.float32)
        own = (1.0 - 3.0 * step_size) - step_size * at(potential, plane_cells_at, offset, BLOCK)
        return own * v + (0.5 * step_size) * total

    def ends(p):
        x = step * planes + p
        return (jnp.where(x > 0, 1.0, 0.0), jnp.where(x + 1 < size_x, 1.0, 0.0))

    @pl.when(index == 0)
    def _():
        filled = jnp.clip(per_device - first_place, 0, pl.num_programs(1))
        filled = filled * planes * groups * (8 * size_z)

        def clear(k, carry):
            lane = pl.multiple_of(k * LANES, LANES)
            out[0, :, pl.ds(lane, LANES)] = jnp.zeros((rows, LANES), out.dtype)
            return carry

        lax.fori_loop(filled // LANES, width // LANES, clear, 0)

    depth = blocks * BLOCK // GROUP
    segments = ((0, depth // 2), (depth // 2, depth * 3 // 4), (depth * 3 // 4, depth))
    doubled = jnp.where(size_z == 32, 2, 1)

    @pl.when(live)
    def _():
        for p in range(planes):
            beside = in_plane(p)
            below_on, above_on = ends(p)
            target = (index * planes + p) * groups * (8 * size_z)
            for first, last in segments:

                @pl.when(first < groups)
                def _(first=first, last=last):
                    for b in range(first * GROUP // BLOCK, last * GROUP // BLOCK):
                        value = trial_block(p, beside, b, below_on, above_on)
                        held[:, b * BLOCK : (b + 1) * BLOCK] = value.astype(held.dtype)

            @pl.when(size_z == BOX)
            def _():
                def group_copy(group, carry):
                    lane = pl.multiple_of(target + group * GROUP, GROUP)
                    base = pl.multiple_of(group * GROUP, GROUP)
                    out[0, :, pl.ds(lane, GROUP)] = held[:, pl.ds(base, GROUP)]
                    return carry

                lax.fori_loop(0, groups, group_copy, 0)

            @pl.when(size_z < BOX)
            def _():
                for j in range(3):
                    begin = (j if j != 1 else doubled) * LANES
                    picked = []
                    for group in range(depth):
                        at_lane = begin + group * GROUP
                        if j == 1:
                            at_lane = pl.multiple_of(at_lane, LANES)
                        picked.append(held[:, pl.ds(at_lane, BLOCK)])
                    packed = jnp.dot(stack(picked), packing[0, j], preferred_element_type=jnp.float32)

                    @pl.when((size_z == 48) | (j < 2))
                    def _(j=j, packed=packed):
                        for first, last in segments:

                            @pl.when(first < groups)
                            def _(first=first, last=last):
                                for group in range(first, last):
                                    lane = target + group * (8 * size_z) + j * LANES
                                    lane = pl.multiple_of(lane, LANES)
                                    value = packed[group * rows : (group + 1) * rows, :]
                                    out[0, :, pl.ds(lane, LANES)] = value.astype(out.dtype)


def stack(pieces):
    if pieces[0].shape[0] % 16:
        pieces = [piece.astype(jnp.float32) for piece in pieces]
    return jnp.concatenate(pieces, axis=0).astype(jnp.bfloat16)


def packing_table(size_z):
    j = np.arange(3)[:, None, None]
    k = np.arange(BLOCK)[None, :, None]
    lane = j * LANES + np.arange(LANES)[None, None, :]
    begin = (2 * j if size_z == 32 else j) * LANES
    source = lane // size_z * BOX + lane % size_z - begin
    return (source == k) & (lane < 8 * size_z)


def spreading_table(size_z):
    i = np.arange(2)[:, None, None]
    k = np.arange(BLOCK)[None, :, None]
    lane = i * BLOCK + np.arange(BLOCK)[None, None, :]
    begin = (i if size_z == 48 else 0) * LANES
    source = lane // BOX * size_z + lane % BOX - begin
    return (source == k) & (lane % BOX < size_z)


def in_plane_stencil(size_z):
    source = np.arange(2 * BLOCK)[:, None] - LANES
    target = np.arange(BLOCK)[None, :]
    along_y = np.abs(source - target) == BOX
    along_z = (np.abs(source - target) == 1) & ((source + LANES) // BOX == (target + LANES) // BOX)
    return (along_y | along_z) & ((source + LANES) % BOX < size_z)


def tables_of(make):
    return jnp.asarray(np.stack([make(z) for z in (32, 48, 64)]), jnp.bfloat16)


def level(size_z):
    return size_z // 16 - 2


def packed_trial(wave, potential, stencil, packing, sizes, first_place, places, width, band_count):
    rows = wave.shape[0]
    planes, parts = step_plan(band_count)
    plane_cells = BOX * BOX

    def step(i, j, sizes):
        per_device = units_per_device(sizes[0], band_count)
        return (i * per_device + jnp.minimum(first_place + j, per_device - 1)) // parts

    def plane(shift):
        return lambda i, j, s: (0, jnp.clip(step(i, j, s) * planes + shift, 0, s[0] - 1))

    share = places * planes * plane_cells * band_count // parts
    return pl.pallas_call(
        functools.partial(trial_kernel, planes, parts, first_place),
        out_shape=jax.ShapeDtypeStruct((band_count, rows, width), jnp.bfloat16),
        grid_spec=pltpu.PrefetchScalarGridSpec(
            num_scalar_prefetch=1,
            grid=(band_count, places),
            in_specs=[
                pl.BlockSpec((rows, plane_cells), plane(-1)),
                pl.BlockSpec((rows, planes * plane_cells), lambda i, j, s: (0, step(i, j, s))),
                pl.BlockSpec((rows, plane_cells), plane(planes)),
                pl.BlockSpec((1, planes * plane_cells), lambda i, j, s: (0, step(i, j, s))),
                pl.BlockSpec((1, 2 * BLOCK, BLOCK), lambda i, j, s: (level(s[2]), 0, 0)),
                pl.BlockSpec((1, 3, BLOCK, LANES), lambda i, j, s: (level(s[2]), 0, 0, 0)),
            ],
            out_specs=pl.BlockSpec((1, rows, width), lambda i, j, s: (i, 0, 0)),
            scratch_shapes=[pltpu.VMEM((rows, plane_cells // parts), jnp.bfloat16)],
        ),
        compiler_params=pltpu.CompilerParams(vmem_limit_bytes=40 << 20),
        cost_estimate=pl.CostEstimate(
            flops=1024 * rows * share, bytes_accessed=6 * rows * share, transcendentals=0
        ),
        name="packed_trial",
    )(sizes, wave, wave, wave, potential, stencil, packing)


def unpack_kernel(planes, parts, plane_cells, sizes, owner, local, head, tail, spreading, out):
    step, part = pl.program_id(0), pl.program_id(1)
    size_x, size_y, size_z = sizes[0], sizes[1], sizes[2]
    place = local[step * parts + part]
    groups = size_y // (8 * parts)
    rows = out.shape[0]
    live = step * planes < size_x
    source = jnp.maximum(place - 1, 0) * planes * groups * (8 * size_z)

    @pl.when((part == 0) & ((size_y * BOX < plane_cells) | ~live))
    def _():
        def clear(k, carry):
            out[:, pl.ds(pl.multiple_of(k * GROUP, GROUP), GROUP)] = jnp.zeros(
                (rows, GROUP), out.dtype
            )
            return carry

        lax.fori_loop(0, planes * plane_cells // GROUP, clear, 0)

    def copy_from(packed):
        for p in range(planes):

            def group_copy(group, carry):
                base = pl.multiple_of(p * plane_cells + (part * groups + group) * GROUP, GROUP)
                at = pl.multiple_of(source + (p * groups + group) * GROUP, GROUP)
                out[:, pl.ds(base, GROUP)] = packed[0, :, pl.ds(at, GROUP)]
                return carry

            lax.fori_loop(0, groups, group_copy, 0)

    depth = plane_cells // (GROUP * parts)
    segments = ((0, depth // 2), (depth // 2, depth * 3 // 4), (depth * 3 // 4, depth))
    if depth % 4:
        segments = ((k, k + 1) for k in range(depth))

    def spread_from(packed):
        last_lane = packed.shape[2] - BLOCK
        for p in range(planes):
            for i in range(2):
                shift = jnp.where(size_z == 48, i, 0) * LANES
                picked = []
                for group in range(depth):
                    at = source + (p * groups + group) * (8 * size_z) + shift
                    at = pl.multiple_of(jnp.minimum(at, last_lane), LANES)
                    picked.append(packed[0, :, pl.ds(at, BLOCK)])
                spread = jnp.dot(stack(picked), spreading[0, i], preferred_element_type=jnp.float32)
                for first, last in segments:

                    @pl.when(first < groups)
                    def _(first=first, last=last, spread=spread, i=i, p=p):
                        for group in range(first, last):
                            lane = p * plane_cells + (part * groups + group) * GROUP + i * BLOCK
                            lane = pl.multiple_of(lane, BLOCK)
                            value = spread[group * rows : (group + 1) * rows, :]
                            out[:, pl.ds(lane, BLOCK)] = value.astype(out.dtype)

    for packed, chosen in ((head, place == 0), (tail, place > 0)):
        pl.when(live & chosen & (size_z == BOX))(functools.partial(copy_from, packed))
        pl.when(live & chosen & (size_z < BOX))(functools.partial(spread_from, packed))


def unpacked(head, tail, spreading, sizes, owner, local, steps, planes, parts, plane_cells):
    rows = head.shape[1]

    def owned(i, j, s, o, l):
        return (o[i * parts + j], 0, 0)

    return pl.pallas_call(
        functools.partial(unpack_kernel, planes, parts, plane_cells),
        out_shape=jax.ShapeDtypeStruct((rows, steps * planes * plane_cells), head.dtype),
        grid_spec=pltpu.PrefetchScalarGridSpec(
            num_scalar_prefetch=3,
            grid=(steps, parts),
            in_specs=[
                pl.BlockSpec((1, rows, head.shape[2]), owned),
                pl.BlockSpec((1, rows, tail.shape[2]), owned),
                pl.BlockSpec((1, 2, BLOCK, BLOCK), lambda i, j, s, o, l: (level(s[2]), 0, 0, 0)),
            ],
            out_specs=pl.BlockSpec((rows, planes * plane_cells), lambda i, j, s, o, l: (0, i)),
        ),
        compiler_params=pltpu.CompilerParams(vmem_limit_bytes=40 << 20),
        cost_estimate=pl.CostEstimate(
            flops=0, bytes_accessed=4 * rows * steps * planes * plane_cells, transcendentals=0
        ),
        name="unpacked",
    )(sizes, owner, local, head, tail, spreading)


def laid_kernel(planes, band_count, sizes, head, tail, out):
    unit = pl.program_id(0)
    per_device = sizes[0] // (planes * band_count)
    place = unit - jnp.minimum(unit // per_device, band_count - 1) * per_device
    live = unit * planes < sizes[0]

    @pl.when(live & (place == 0))
    def _():
        out[...] = head[0]

    @pl.when(live & (place > 0))
    def _():
        out[...] = tail[0]

    @pl.when(unit * planes >= sizes[0])
    def _():
        out[...] = jnp.zeros_like(out)


def laid_out(head, tail, sizes, steps, planes):
    band_count, rows = head.shape[:2]
    cells = planes * BOX * BOX

    def owner_of(unit, sizes):
        return jnp.minimum(unit // (sizes[0] // (planes * band_count)), band_count - 1)

    def rest_of(unit, sizes):
        per_device = sizes[0] // (planes * band_count)
        place = unit - owner_of(unit, sizes) * per_device
        return jnp.clip(place - 1, 0, per_device - 2)

    return pl.pallas_call(
        functools.partial(laid_kernel, planes, band_count),
        out_shape=jax.ShapeDtypeStruct((rows, steps * cells), head.dtype),
        grid_spec=pltpu.PrefetchScalarGridSpec(
            num_scalar_prefetch=1,
            grid=(steps,),
            in_specs=[
                pl.BlockSpec((1, rows, cells), lambda i, s: (owner_of(i, s), 0, 0)),
                pl.BlockSpec((1, rows, cells), lambda i, s: (owner_of(i, s), 0, rest_of(i, s))),
            ],
            out_specs=pl.BlockSpec((rows, cells), lambda i, s: (0, i)),
        ),
        compiler_params=pltpu.CompilerParams(vmem_limit_bytes=40 << 20),
        cost_estimate=pl.CostEstimate(
            flops=0, bytes_accessed=4 * rows * steps * cells, transcendentals=0
        ),
        name="laid_out",
    )(sizes, head, tail)


def gram_kernel(count, scale, partial_value, out, landing, whole, sent, landed, shared, spread):
    me = lax.axis_index("band")
    rows = NB // count
    steps = range(1, count)

    def peer(step):
        return {"band": lax.rem(me + step, count)}

    def block(owner):
        return pl.ds(pl.multiple_of(owner * rows, 8), rows)

    barrier = pltpu.get_barrier_semaphore()
    for step in steps:
        pl.semaphore_signal(
            barrier, inc=1, device_id=peer(step), device_id_type=pl.DeviceIdType.MESH
        )
    pl.semaphore_wait(barrier, count - 1)
    out_copies = []
    for step in steps:
        copy = pltpu.make_async_remote_copy(
            src_ref=partial_value.at[block(lax.rem(me + step, count)), :],
            dst_ref=landing.at[step - 1],
            send_sem=sent.at[step - 1],
            recv_sem=landed.at[step - 1],
            device_id=peer(step),
            device_id_type=pl.DeviceIdType.MESH,
        )
        copy.start()
        out_copies.append(copy)
    total = partial_value[block(me), :]
    for step in steps:
        out_copies[step - 1].wait_recv()
        total = total + landing[step - 1]
    whole[block(me), :] = total * scale
    back_copies = []
    for step in steps:
        copy = pltpu.make_async_remote_copy(
            src_ref=whole.at[block(me), :],
            dst_ref=whole.at[block(me), :],
            send_sem=shared.at[step - 1],
            recv_sem=spread.at[step - 1],
            device_id=peer(step),
            device_id_type=pl.DeviceIdType.MESH,
        )
        copy.start()
        back_copies.append(copy)
    for copy in back_copies:
        copy.wait_recv()
    for copy in out_copies + back_copies:
        copy.wait_send()
    out[...] = whole[...]


def summed(partial_value, band_count, scale):
    rows = NB // band_count
    sems = pltpu.SemaphoreType.DMA((band_count - 1,))
    return pl.pallas_call(
        functools.partial(gram_kernel, band_count, scale),
        out_shape=jax.ShapeDtypeStruct((NB, NB), jnp.float32),
        in_specs=[pl.BlockSpec(memory_space=pltpu.VMEM)],
        out_specs=pl.BlockSpec(memory_space=pltpu.VMEM),
        scratch_shapes=[
            pltpu.VMEM((band_count - 1, rows, NB), jnp.float32),
            pltpu.VMEM((NB, NB), jnp.float32),
            sems,
            sems,
            sems,
            sems,
        ],
        compiler_params=pltpu.CompilerParams(collective_id=0, has_side_effects=True),
        name="gram_sum",
    )(partial_value)


def hits(position, extent):
    return position[..., None] == jnp.arange(extent)


def patched_grid(shares, box_sizes, box_offsets, patch_signs, band_count, slots, planes, parts):
    per_device = units_per_device(box_sizes[:, 0], band_count)[:, None, None, None]
    place = jnp.arange(slots)[None, None, :, None]
    unit = jnp.arange(band_count)[None, :, None, None] * per_device + place
    plane = jnp.arange(planes)[None, None, None, :]
    x = jnp.where(place < per_device, unit * planes // parts + plane, -G)
    x = x + box_offsets[:, 0][:, None, None, None]
    pair = LANES // BOX
    depth = BOX // (parts * pair)
    y = jnp.arange(depth)[None, :] * pair
    lane = jnp.arange(LANES)[None, :]
    fragments = box_sizes.shape[0]
    half = jnp.bfloat16
    cube = shares.reshape(fragments, -1, LANES)
    slabs, rows_of = [], []
    for odd in range(pair):
        z = jnp.where(lane // BOX == odd, box_offsets[:, 2][:, None] + lane % BOX, -G)
        along_z = hits(z, G).astype(half)
        wide = lax.dot_general(
            cube, along_z, (((2,), (1,)), ((0,), (0,))), preferred_element_type=half
        ).reshape(fragments, -1, depth, G)
        for part in range(parts):
            own = jnp.where(unit % parts == part, x, -G).reshape(fragments, -1)
            along_x = (hits(own, G) * patch_signs[:, None, None]).astype(half)
            slabs.append(
                lax.dot_general(
                    along_x, wide, (((1,), (1,)), ((0,), (0,))), preferred_element_type=half
                )
            )
            length = (box_sizes[:, 1] // parts)[:, None]
            row = box_offsets[:, 1][:, None] + part * length + y + odd
            rows_of.append(hits(jnp.where(y + odd < length, row, -G), G).astype(half))
    total = lax.dot_general(
        jnp.stack(rows_of, 1),
        jnp.stack(slabs, 1),
        (((0, 1, 2), (0, 1, 3)), ((), ())),
        preferred_element_type=jnp.float32,
    )
    return total.transpose(1, 0, 2)


def hartree_of(patched, table, eigen):
    precise = lax.Precision.HIGH
    spectrum = jnp.einsum("abc,ci->abi", patched, table, precision=precise)
    spectrum = jnp.einsum("abc,bi->aic", spectrum, table, precision=precise)
    spectrum = jnp.einsum("abc,ai->ibc", spectrum, table, precision=precise)
    spectrum = spectrum * (
        screening
        / (eigen[:, None, None] + eigen[None, :, None] + eigen[None, None, :] + screening)
    )
    spectrum = jnp.einsum("abc,ai->ibc", spectrum, table, precision=precise)
    spectrum = jnp.einsum("abc,bi->aic", spectrum, table, precision=precise)
    return jnp.einsum("abc,ci->abi", spectrum, table, precision=precise)


def total_of(hartree, patched):
    return hartree - local_factor * jnp.cbrt(jnp.maximum(patched, 0.0))


def widened(block, width):
    return jnp.pad(block, ((0, 0),) * (block.ndim - 1) + ((0, width - block.shape[-1]),))


def chosen(choice, branches, *operands):
    if len(branches) == 1:
        return branches[0](*operands)
    half = len(branches) // 2 if len(branches) < 4 else 1
    return lax.cond(
        choice < half,
        lambda *given: chosen(choice, branches[:half], *given),
        lambda *given: chosen(choice - half, branches[half:], *given),
        *operands,
    )


def swapped(blocks):
    return lax.all_to_all(blocks, "band", split_axis=0, concat_axis=0, tiled=True)


def body(wave_coeffs, old_potential, occupations, box_sizes, box_offsets, patch_signs):
    fragment = lax.axis_index("frag")
    band_index = lax.axis_index("band")
    band_count = lax.axis_size("band")
    planes, parts = step_plan(band_count)
    cells = BOX * BOX * BOX
    cell_volume = 1.0 / BOX**3
    sizes_here = lax.dynamic_index_in_dim(box_sizes, fragment, 0, keepdims=False)
    offsets_here = lax.dynamic_index_in_dim(box_offsets, fragment, 0, keepdims=False)
    axis = jnp.arange(BOX)
    mask = (
        (axis < sizes_here[0])[:, None, None]
        & (axis < sizes_here[1])[None, :, None]
        & (axis < sizes_here[2])[None, None, :]
    )
    owner, local = live_units(sizes_here, band_count)
    widths = class_widths(band_count)
    room = tuple(max(pair) for pair in zip(*widths))
    volume = sizes_here[0] * sizes_here[1] * sizes_here[2] * 64
    tops = jnp.array([top * BOX**3 for top in CLASSES], jnp.int32)
    choice = jnp.sum((volume <= tops).astype(jnp.int32)) - 1
    unit_cells = BOX * BOX // parts
    slots = units_per_device(BOX, band_count)
    share_sizes = jnp.stack(
        [units_per_device(sizes_here[0], band_count) * planes, sizes_here[1] // parts, sizes_here[2]]
    )
    share_owner = jnp.zeros(slots, jnp.int32)
    share_local = jnp.arange(slots, dtype=jnp.int32)

    stencil = tables_of(in_plane_stencil)
    packing = tables_of(packing_table)
    spreading = tables_of(spreading_table)

    def forward(pair):
        def branch(wave, potential):
            rows, partial_value = [], 0.0
            places = ((0, 1), (1, slots - 1))
            for (first, count), width, space in zip(places, pair, room):
                trial = packed_trial(
                    wave, potential, stencil, packing, sizes_here, first, count, width, band_count
                )
                part = swapped(trial).reshape(NB, width)
                gram = lax.dot_general(
                    part, part, (((1,), (1,)), ((), ())), preferred_element_type=jnp.float32
                )
                partial_value = lax.optimization_barrier(partial_value + gram)
                rows.append(widened(part, space))
            return (rows[0], rows[1], partial_value)

        return branch

    head, tail, partial_value = chosen(
        choice, [forward(pair) for pair in widths], wave_coeffs[0], old_potential
    )
    gram = summed(partial_value, band_count, cell_volume)
    coeff = newton_schulz(gram)

    sent, density = [], []
    for rows, width in zip((head, tail), room):
        fresh = lax.dot_general(
            coeff, rows, (((0,), (0,)), ((), ())), preferred_element_type=jnp.float32
        )
        value = jnp.sum(occupations[0][:, None] * fresh * fresh, axis=0) / NB
        density.append(jnp.broadcast_to(value.astype(jnp.bfloat16), (1, 8, width)))
        sent.append(fresh.astype(jnp.bfloat16).reshape(band_count, NB // band_count, width))
    sent_head, sent_tail = sent
    share = unpacked(
        density[0],
        density[1],
        spreading,
        share_sizes,
        share_owner,
        share_local,
        slots,
        planes,
        1,
        unit_cells,
    )
    share = share[0].reshape(-1, LANES)
    shares = lax.all_gather(share, ("frag", "band"), axis=0, tiled=True)

    def early(pair):
        def branch(sent):
            return widened(swapped(sent[:, :, : pair[0]]), room[0])

        return branch

    back_head = lax.switch(choice, [early(pair) for pair in widths], sent_head)

    table, eigen = lax.optimization_barrier(sine_table())

    rests = sorted({rest for _, rest in widths}, reverse=True)
    rests = [rest for k, rest in enumerate(rests) if k in (0, 1, 2, 4, 6)]
    rest_here = (units_per_device(sizes_here[0], band_count) - 1) * planes
    rest_here = rest_here * (sizes_here[1] // parts) * sizes_here[2]
    late_choice = jnp.sum((rest_here <= jnp.array(rests)).astype(jnp.int32)) - 1

    def late(rest):
        def branch(sent, shares):
            back = swapped(sent[:, :, :rest])
            patched = patched_grid(
                shares, box_sizes, box_offsets, patch_signs, band_count, slots, planes, parts
            )
            hartree = hartree_of(patched, table, eigen)

            def slab_of(grid):
                rows = G // band_count
                return lax.dynamic_slice_in_dim(grid, band_index * rows, rows)

            def window_of(grid):
                extended = jnp.pad(grid, ((0, BOX), (0, BOX), (0, BOX)))
                return lax.dynamic_slice(
                    extended, (offsets_here[0], offsets_here[1], offsets_here[2]), (BOX, BOX, BOX)
                )

            slab = total_of(slab_of(hartree), slab_of(patched))
            window = total_of(window_of(hartree), window_of(patched))
            window = jnp.where(mask, window, 0.0).reshape(1, cells)
            return (widened(back, room[1]), window, slab)

        return branch

    back_tail, window, slab = chosen(
        late_choice, [late(rest) for rest in rests], sent_tail, shares
    )
    def spread_out(head, tail):
        return unpacked(
            head,
            tail,
            spreading,
            sizes_here,
            owner,
            local,
            BOX // planes,
            planes,
            parts,
            BOX * BOX,
        )

    if parts == 1:
        waves_out = lax.cond(
            (sizes_here[1] < BOX) | (sizes_here[2] < BOX),
            spread_out,
            lambda head, tail: laid_out(head, tail, sizes_here, BOX // planes, planes),
            back_head,
            back_tail,
        )
    else:
        waves_out = spread_out(back_head, back_tail)
    return (waves_out[None], window, slab)


def solution(mesh):
    placed = (P("frag", "band", None), P("frag", None), P("frag", None), P(), P(), P())
    return jax.shard_map(
        body,
        mesh=mesh,
        in_specs=placed,
        out_specs=(P("frag", "band", None), P("frag", None), P("band", None, None)),
        check_vma=False,
    )
```
